128 devices in a mesh: fx: 8 (over y_hi, z), fy: 16 (over x, y_lo, core).
Axes of the slice: x: 4, y: 4 (y_hi: 2, y_lo: 2; y = y_hi * 2 + y_lo), z: 4, core: 2. Of those that a mesh axis runs over, the one named last changes fastest.
Arguments:
- facets: float32 [8192, 4096], P('fx', 'fy'), may hold values from -6 to 6
- counts: int32 [8, 16], P('fx', 'fy'), may hold values from 1 to 16, as said below
- cells: int32 [2, 8, 16, 2048], P(None, 'fx', 'fy'), may hold values from 0 to 248
- fracs: float32 [2, 8, 16, 2048], P(None, 'fx', 'fy'), may hold values from 0 to 1
Outputs:
- predictions: float32 [2, 8, 16, 2048], P(None, 'fx', 'fy')
The draws below stay inside these ranges and needn't reach their ends.
Inputs may be any that keep to these rules, and one draw needn't show every extreme that they name: Blocks 0 to counts - 1 of a subgrid's 128-visibility blocks are live, the others are padding; some subgrid has 16 live blocks.
All inputs are finite; a program needn't handle non-finite values.
Results may differ from the reference program's by a relative error of at most 0.0003.
Values sent between devices are 32-bit elements; how exact they have to be, the bound alone decides.
A program may use at most 128 MiB of HBM per device.

```python
import math
import jax
import jax.numpy as jnp
from jax import lax

NIMG = 65536
FP = 4096
SUBGRID = 256
SUPPORT = 8
VBLOCK = 128
MAXB = 16
WROWS = 8192
WCOLS = 4096
NSU = 8
NSV = 16
NVIS = 2048


def draw_counts(key, part):
    key_heavy, key_big, key_small, key_spot = jax.random.split(jax.random.fold_in(key, 11), 4)
    heavy = jax.random.randint(key_heavy, (NSU, NSV), 0, 4) == 0
    big = jax.random.randint(key_big, (NSU, NSV), MAXB // 2, MAXB + 1)
    small = jax.random.randint(key_small, (NSU, NSV), 1, MAXB // 4 + 1)
    loads = jnp.where(heavy, big, small).reshape(-1)
    spot = jax.random.randint(key_spot, (), 0, NSU * NSV)
    loads = jnp.where(jnp.arange(NSU * NSV, dtype=jnp.int32) == spot, MAXB, loads)
    return loads.reshape(NSU, NSV).astype(jnp.int32)


def set_ends(array, stream_key, smallest, largest):
    extent = array.shape
    index_at = [jax.random.randint(jax.random.fold_in(stream_key, axis), (), 0, extent[axis]) for axis in range(len(extent))]
    array = array.at[tuple(index_at)].set(smallest)
    longest = extent.index(max(extent))
    index_at[longest] = (index_at[longest] + 1) % extent[longest]
    return array.at[tuple(index_at)].set(largest)


def block_levels(rng, dims, cuts, low, high):
    level, own = 1.0, jax.random.fold_in(rng, 6)
    for axis_at, blocks in cuts:
        draws = jnp.exp(jax.random.uniform(jax.random.fold_in(own, axis_at), (blocks,), jnp.float32, low / len(cuts), high / len(cuts)))
        level = level * jnp.repeat(draws, dims[axis_at] // blocks).reshape([-1 if axis == axis_at else 1 for axis in range(len(dims))])
    return level


def centred(rng, dims, deviation, limit, cuts=(), held_as=jnp.bfloat16):
    factor_of = block_levels(rng, dims, cuts, -0.22, 0.18) if cuts else 1.0
    drawn = jax.random.normal(rng, dims, jnp.float32) * deviation * factor_of
    return jnp.minimum(jnp.maximum(drawn, -limit), limit).astype(held_as)


def setup_inputs(seed: int = 0) -> dict:
    keys = jax.random.split(jax.random.key(seed), 5)
    return {
        "facets": centred(keys[0], (WROWS, WCOLS), 1.0, 6.0, ((0, 8), (1, 16)), jnp.float32),
        "counts": draw_counts(jax.random.fold_in(keys[4], 71), 0),
        "cells": set_ends(jax.random.randint(keys[2], (2, NSU, NSV, NVIS), 0, SUBGRID - SUPPORT + 1), jax.random.fold_in(keys[2], 1), 0, SUBGRID - SUPPORT).astype(jnp.int32),
        "fracs": jnp.clip(1.0 * jax.random.uniform(keys[3], (2, NSU, NSV, NVIS), jnp.float32) ** block_levels(keys[3], (2, NSU, NSV, NVIS), ((1, 8), (2, 16)), -0.2, 0.2), 0.0, 1.0),
    }


def mulmod(upper, lower):
    low = upper % 256
    high = upper // 256
    return (low * lower + 256 * (high * lower % (NIMG // 256))) % NIMG

def factor(freqs, pixels, scale):
    inner = pixels % FP
    turns = mulmod(freqs[:, None], pixels[None, :])
    angle = turns.astype(jnp.float32) * (2.0 * math.pi / NIMG)
    window = jnp.sin(math.pi * (inner.astype(jnp.float32) + 0.5) / FP) * scale
    return (jnp.cos(angle) * window[None, :], -jnp.sin(angle) * window[None, :])

def kernel(offset, frac):
    positions = jnp.arange(SUBGRID, dtype=jnp.int32)
    dist = positions[None, :] - offset[:, None]
    inside = (dist >= 0) & (dist < SUPPORT)
    shift = dist.astype(jnp.float32) - (SUPPORT // 2 - 1) - frac[:, None]
    value = 0.6 * jnp.exp(-shift * shift / 4.5)
    return jnp.where(inside, value, jnp.zeros_like(value))

def reference(facets, counts, cells, fracs):
    highest = lax.Precision.HIGHEST
    row_scale = math.sqrt(2.0 / WROWS)
    col_scale = math.sqrt(2.0 / WCOLS)
    rows_all = jnp.arange(WROWS, dtype=jnp.int32)
    cols_all = jnp.arange(WCOLS, dtype=jnp.int32)

    def first(index):
        freqs = index * SUBGRID + jnp.arange(SUBGRID, dtype=jnp.int32)
        real_part, imag_part = factor(freqs, rows_all, row_scale)
        return jnp.stack([jnp.dot(real_part, facets, precision=highest, preferred_element_type=jnp.float32), jnp.dot(imag_part, facets, precision=highest, preferred_element_type=jnp.float32)])
    partial_sums = lax.map(first, jnp.arange(NSU, dtype=jnp.int32))
    p_real = partial_sums[:, 0].reshape(NSU * SUBGRID, WCOLS)
    p_imag = partial_sums[:, 1].reshape(NSU * SUBGRID, WCOLS)

    def second(index):
        freqs = index * SUBGRID + jnp.arange(SUBGRID, dtype=jnp.int32)
        b_real, b_imag = factor(freqs, cols_all, col_scale)
        rr = jnp.dot(b_real, p_real.T, precision=highest, preferred_element_type=jnp.float32)
        ii = jnp.dot(b_imag, p_imag.T, precision=highest, preferred_element_type=jnp.float32)
        ir = jnp.dot(b_imag, p_real.T, precision=highest, preferred_element_type=jnp.float32)
        ri = jnp.dot(b_real, p_imag.T, precision=highest, preferred_element_type=jnp.float32)
        return jnp.stack([rr - ii, ir + ri])
    grids = lax.map(second, jnp.arange(NSV, dtype=jnp.int32))

    def degrid(index):
        row = index // NSV
        col = index % NSV
        zero = jnp.zeros((), jnp.int32)
        grid = lax.dynamic_slice(grids, (col, zero, zero, row * SUBGRID), (1, 2, SUBGRID, SUBGRID))[0]
        weight_u = kernel(cells[0, row, col], fracs[0, row, col])
        weight_v = kernel(cells[1, row, col], fracs[1, row, col])
        g_real = jnp.dot(weight_v, grid[0], precision=highest, preferred_element_type=jnp.float32)
        g_imag = jnp.dot(weight_v, grid[1], precision=highest, preferred_element_type=jnp.float32)
        v_real = lax.optimization_barrier(jnp.sum(g_real * weight_u, axis=1))
        v_imag = lax.optimization_barrier(jnp.sum(g_imag * weight_u, axis=1))
        live = jnp.arange(NVIS, dtype=jnp.int32) // VBLOCK < counts[row, col]
        return jnp.stack([jnp.where(live, v_real, jnp.zeros_like(v_real)), jnp.where(live, v_imag, jnp.zeros_like(v_imag))])
    values = lax.map(degrid, jnp.arange(NSU * NSV, dtype=jnp.int32))
    return values.reshape(NSU, NSV, 2, NVIS).transpose(2, 0, 1, 3)
```

```python
import functools
import math

import jax
import jax.numpy as jnp
import numpy as np
from jax import lax
from jax.experimental import pallas as pl
from jax.experimental.pallas import tpu as pltpu
from jax.sharding import PartitionSpec as P

NIMG = 65536
FP = 4096
SUB = 256
SUPPORT = 8
VBLOCK = 128
MESH = pl.DeviceIdType.MESH
BF = jnp.bfloat16
F32 = jnp.float32


def separable(cells, pixels, rank):
    a = np.arange(cells) - (cells - 1) / 2
    b = np.arange(pixels) - (pixels - 1) / 2
    theta = 2 * np.pi * np.outer(a, b) / NIMG
    half = rank // 2
    uc, sc, vc = np.linalg.svd(np.cos(theta), full_matrices=False)
    us, ss, vs = np.linalg.svd(np.sin(theta), full_matrices=False)
    left = np.concatenate([uc[:, :half] * sc[:half], -1j * us[:, :half] * ss[:half]], axis=1)
    right = np.concatenate([vc[:half], vs[:half]], axis=0)
    norm = math.sqrt(pixels)
    return left / norm, right * norm


def axis_tables(parts, pixels, subs, rank):
    left, right = separable(SUB, pixels, rank)
    right = right * math.sqrt(2.0 / (parts * pixels))
    xx = np.arange(pixels)
    mid = SUB * np.arange(subs) + (SUB - 1) / 2
    phase = 2 * np.pi * ((mid[:, None] * xx[None, :]) / NIMG)
    turn = np.concatenate([np.cos(phase), -np.sin(phase)], axis=0)
    x = np.arange(parts * pixels)
    window = np.sin(np.pi * ((x % FP) + 0.5) / FP).reshape(parts, pixels)
    kk = np.arange(SUB)
    at = (kk[:, None] * np.arange(parts)[None, :] * pixels % NIMG) / NIMG
    at = at + ((kk - (SUB - 1) / 2) * ((pixels - 1) / 2) / NIMG)[:, None]
    back = np.exp(-2j * np.pi * at)[:, :, None] * left[:, None, :]
    return turn, right, window, back.reshape(SUB, parts * rank)


def split(x):
    high = x.astype(BF)
    return high, (x - high.astype(F32)).astype(BF)


def mm(a, b, dims):
    return lax.dot_general(a, b, (dims, ((), ())), preferred_element_type=F32)


def mm3(a, b, dims):
    (ah, al), (bh, bl) = a, b
    return mm(ah, bh, dims) + (mm(ah, bl, dims) + mm(al, bh, dims))


NN = ((1,), (0,))
NT = ((1,), (1,))


def weights(offset, frac, shape):
    cell = lax.broadcasted_iota(jnp.int32, shape, 0).astype(F32)
    shift = cell - (offset.astype(F32) + (SUPPORT // 2 - 1))
    inside = jnp.abs(shift - 0.5) < SUPPORT // 2
    shift = shift - frac
    value = 0.6 * jnp.exp(shift * shift * (-1.0 / 4.5))
    return jnp.where(inside, value, 0.0)


def kernel(
    nx, ny, rp, rq, tx_hbm, ty_hbm, back_hbm, f_hbm, counts_hbm, cells_hbm, fracs_hbm, out_ref,
    tx, ty, back, f, counts, cells, fracs, m2, z, r1, t, r2, wv, wu,
    fsem, lsem, s1, v1, s2, v2,
):
    me_x = lax.axis_index("fx")
    me_y = lax.axis_index("fy")
    rows = f.shape[0]
    cols = f.shape[1]
    step = rows // 4

    small = [
        pltpu.make_async_copy(src, dst, lsem.at[i])
        for i, (src, dst) in enumerate(
            [
                (tx_hbm, tx), (ty_hbm, ty), (cells_hbm, cells), (fracs_hbm, fracs),
                (counts_hbm, counts), (back_hbm, back),
            ]
        )
    ]
    big = [
        pltpu.make_async_copy(
            f_hbm.at[pl.ds(i * step, step)], f.at[pl.ds(i * step, step)], fsem.at[i]
        )
        for i in range(4)
    ]
    small[0].start()
    big[0].start()
    small[1].start()
    for copy in big[1:] + small[2:]:
        copy.start()

    barrier = pltpu.get_barrier_semaphore()
    for d in range(1, nx):
        pl.semaphore_signal(
            barrier, inc=1, device_id=(lax.rem(me_x + d, nx), me_y), device_id_type=MESH
        )
    for d in range(1, ny):
        pl.semaphore_signal(
            barrier, inc=1, device_id=(me_x, lax.rem(me_y + d, ny)), device_id_type=MESH
        )

    small[0].wait()
    wx = tx[pl.ds(2 * nx + rp + me_x, 1), :]
    phi = tx[pl.ds(2 * nx, rp), :] * wx
    c1 = None
    for i in range(4):
        lanes = slice(i * step, (i + 1) * step)
        part = jnp.concatenate(
            [
                jnp.broadcast_to(tx[pl.ds(r, 1), lanes], (rp, step)) * phi[:, lanes]
                for r in range(2 * nx)
            ],
            axis=0,
        )
        big[i].wait()
        prod = mm3(split(part), split(f[pl.ds(i * step, step), :]), NN)
        c1 = prod if c1 is None else c1 + prod

    small[1].wait()
    wy = ty[pl.ds(2 * ny + rq + me_y, 1), :]
    phi = ty[pl.ds(2 * ny, rq), :] * wy
    for r in range(2 * ny):
        m2[pl.ds(r * rq, rq), :] = jnp.broadcast_to(ty[pl.ds(r, 1), :], (rq, cols)) * phi
    prod = mm3(split(c1), split(m2[...]), NT)
    hx = nx * rp
    hy = ny * rq
    z[0] = (prod[:hx, :hy] - prod[hx:, hy:]).reshape(nx, rp, hy)
    z[1] = (prod[:hx, hy:] + prod[hx:, :hy]).reshape(nx, rp, hy)

    pl.semaphore_wait(barrier, nx + ny - 2)
    first = []
    for d in range(1, nx):
        peer = lax.rem(me_x + d, nx)
        copy = pltpu.make_async_remote_copy(
            src_ref=z.at[:, peer], dst_ref=r1.at[:, me_x], send_sem=s1.at[d], recv_sem=v1.at[d],
            device_id=(peer, me_y), device_id_type=MESH,
        )
        copy.start()
        first.append(copy)
    r1[:, pl.ds(me_x, 1)] = z[:, pl.ds(me_x, 1)]

    for copy in small[2:5]:
        copy.wait()
    nvis = cells.shape[3]
    wide = 256
    chunks = nvis // wide

    def fill_v(j, carry):
        at = pl.ds(pl.multiple_of(j * wide, wide), wide)
        high, low = split(weights(cells[1, 0, :, at], fracs[1, 0, :, at], (SUB, wide)))
        wv[0, :, at] = high
        wv[1, :, at] = low
        return carry

    lax.fori_loop(0, chunks, fill_v, 0)

    for copy in first:
        copy.wait()
    for c in range(2):
        t[:, :, c * hx : (c + 1) * hx] = r1[c].reshape(hx, hy).T.reshape(ny, rq, hx)
    second = []
    for d in range(1, ny):
        peer = lax.rem(me_y + d, ny)
        copy = pltpu.make_async_remote_copy(
            src_ref=t.at[peer], dst_ref=r2.at[me_y], send_sem=s2.at[d], recv_sem=v2.at[d],
            device_id=(me_x, peer), device_id_type=MESH,
        )
        copy.start()
        second.append(copy)
    r2[pl.ds(me_y, 1)] = t[pl.ds(me_y, 1)]

    def fill_u(j, carry):
        at = pl.ds(pl.multiple_of(j * wide, wide), wide)
        wu[:, at] = weights(cells[0, 0, :, at], fracs[0, 0, :, at], (SUB, wide))
        return carry

    lax.fori_loop(0, chunks, fill_u, 0)
    small[5].wait()

    for copy in second:
        copy.wait()
    got = r2[...].reshape(hy, 2 * hx)
    g_re = got[:, :hx]
    g_im = got[:, hx:]
    g2 = jnp.concatenate(
        [jnp.concatenate([g_re, g_im], axis=1), jnp.concatenate([-g_im, g_re], axis=1)], axis=0
    )
    kx = 2 * hx
    ky = 2 * hy
    vt = (back[2 * SUB : 3 * SUB, :ky], back[2 * SUB : 3 * SUB, ky : 2 * ky])
    ut = (back[: 2 * SUB, :kx], back[: 2 * SUB, kx : 2 * kx])
    half = mm3(vt, split(g2), NN)
    gh, gl = split(mm3(ut, split(half), NT))
    live = counts[...]

    def degrid(j, carry):
        at = pl.ds(pl.multiple_of(j * wide, wide), wide)
        wh = wv[0, :, at]
        wl = wv[1, :, at]
        sums = mm3((gh, gl), (wh, wl), NN)
        w = wu[:, at]
        block = (lax.broadcasted_iota(jnp.int32, (1, wide), 1) + j * wide) // VBLOCK
        alive = block < live
        re = jnp.sum(sums[:SUB] * w, axis=0, keepdims=True)
        im = jnp.sum(sums[SUB:] * w, axis=0, keepdims=True)
        out_ref[0, 0, :, at] = jnp.where(alive, re, 0.0)
        out_ref[1, 0, :, at] = jnp.where(alive, im, 0.0)
        return carry

    lax.fori_loop(0, chunks, degrid, 0)


def solution(mesh):
    nx = mesh.shape["fx"]
    ny = mesh.shape["fy"]
    rp, rq = 16, 8

    def per_device(facets, counts, cells, fracs):
        rows, cols = facets.shape
        nvis = cells.shape[3]
        turn_x, right_x, win_x, back_x = axis_tables(nx, rows, nx, rp)
        turn_y, right_y, win_y, back_y = axis_tables(ny, cols, ny, rq)
        tx = jnp.asarray(np.concatenate([turn_x, right_x, win_x]), F32)
        ty = jnp.asarray(np.concatenate([turn_y, right_y, win_y]), F32)
        back = np.concatenate(
            [
                np.concatenate([back_x.real, -back_x.imag], axis=1),
                np.concatenate([back_x.imag, back_x.real], axis=1),
                np.concatenate([back_y.real, back_y.imag], axis=1),
            ]
        ).astype(np.float32)
        high = back.astype(BF)
        low = (back - high.astype(np.float32)).astype(BF)
        back = jnp.asarray(np.concatenate([high, low], axis=1))
        hx, hy = nx * rp, ny * rq
        any_spec = pl.BlockSpec(memory_space=pltpu.HBM)
        dma = pltpu.SemaphoreType.DMA
        return pl.pallas_call(
            functools.partial(kernel, nx, ny, rp, rq),
            out_shape=jax.ShapeDtypeStruct((2, 1, 1, nvis), F32),
            in_specs=[any_spec] * 7,
            out_specs=pl.BlockSpec(memory_space=pltpu.VMEM),
            scratch_shapes=[
                pltpu.VMEM(tx.shape, F32),
                pltpu.VMEM(ty.shape, F32),
                pltpu.VMEM(back.shape, BF),
                pltpu.VMEM((rows, cols), F32),
                pltpu.VMEM((1, 1), jnp.int32),
                pltpu.VMEM(cells.shape, jnp.int32),
                pltpu.VMEM(fracs.shape, F32),
                pltpu.VMEM((2 * hy, cols), F32),
                pltpu.VMEM((2, nx, rp, hy), F32),
                pltpu.VMEM((2, nx, rp, hy), F32),
                pltpu.VMEM((ny, rq, 2 * hx), F32),
                pltpu.VMEM((ny, rq, 2 * hx), F32),
                pltpu.VMEM((2, SUB, nvis), BF),
                pltpu.VMEM((SUB, nvis), F32),
                dma((4,)),
                dma((6,)),
                dma((nx,)),
                dma((nx,)),
                dma((ny,)),
                dma((ny,)),
            ],
            compiler_params=pltpu.CompilerParams(
                collective_id=0, has_side_effects=True, vmem_limit_bytes=48 << 20
            ),
        )(tx, ty, back, facets, counts, cells, fracs)

    spec = P(None, "fx", "fy", None)
    return jax.shard_map(
        per_device,
        mesh=mesh,
        in_specs=(P("fx", "fy"), P("fx", "fy"), spec, spec),
        out_specs=spec,
        check_vma=False,
    )
```

```python
import functools
import math

import jax
import jax.numpy as jnp
import numpy as np
from jax import lax
from jax.experimental import pallas as pl
from jax.experimental.pallas import tpu as pltpu
from jax.sharding import PartitionSpec as P

NIMG = 65536
FP = 4096
SUB = 256
SUPPORT = 8
VBLOCK = 128
MESH = pl.DeviceIdType.MESH
BF = jnp.bfloat16
F32 = jnp.float32


def separable(cells, pixels, rank):
    a = np.arange(cells) - (cells - 1) / 2
    b = np.arange(pixels) - (pixels - 1) / 2
    theta = 2 * np.pi * np.outer(a, b) / NIMG
    half = rank // 2
    uc, sc, vc = np.linalg.svd(np.cos(theta), full_matrices=False)
    us, ss, vs = np.linalg.svd(np.sin(theta), full_matrices=False)
    left = np.concatenate([uc[:, :half] * sc[:half], -1j * us[:, :half] * ss[:half]], axis=1)
    right = np.concatenate([vc[:half], vs[:half]], axis=0)
    norm = math.sqrt(pixels)
    return left / norm, right * norm


def axis_tables(parts, pixels, subs, rank):
    left, right = separable(SUB, pixels, rank)
    right = right * math.sqrt(2.0 / (parts * pixels))
    xx = np.arange(pixels)
    mid = SUB * np.arange(subs) + (SUB - 1) / 2
    phase = 2 * np.pi * ((mid[:, None] * xx[None, :]) / NIMG)
    turn = np.concatenate([np.cos(phase), -np.sin(phase)], axis=0)
    x = np.arange(parts * pixels)
    window = np.sin(np.pi * ((x % FP) + 0.5) / FP).reshape(parts, pixels)
    kk = np.arange(SUB)
    at = (kk[:, None] * np.arange(parts)[None, :] * pixels % NIMG) / NIMG
    at = at + ((kk - (SUB - 1) / 2) * ((pixels - 1) / 2) / NIMG)[:, None]
    back = np.exp(-2j * np.pi * at)[:, :, None] * left[:, None, :]
    return turn, right, window, back.reshape(SUB, parts * rank)


def split(x):
    high = x.astype(BF)
    return high, (x - high.astype(F32)).astype(BF)


def mm(a, b, dims):
    return lax.dot_general(a, b, (dims, ((), ())), preferred_element_type=F32)


def mm3(a, b, dims):
    (ah, al), (bh, bl) = a, b
    return mm(ah, bh, dims) + (mm(ah, bl, dims) + mm(al, bh, dims))


NN = ((1,), (0,))
NT = ((1,), (1,))
WIDE = 512
UNROLL = 4
FARX = (6, 5, 7, 2, 4, 1, 3)
FARY = (11, 10, 9, 8, 7, 6, 15, 14, 3, 2, 5, 4, 13, 12, 1)


def shift_x(at, d):
    return (at // 4 + d // 4) % 2 * 4 + (at + d) % 4


def shift_y(at, d):
    x = (at // 4 + d // 4) % 4
    near = (at // 2 + d // 2) % 2
    return x * 4 + near * 2 + (at + d) % 2


def weights(offset, frac, shape):
    cell = lax.broadcasted_iota(jnp.int32, shape, 0).astype(F32)
    shift = cell - (offset.astype(F32) + (SUPPORT // 2 - 1))
    inside = jnp.abs(shift - 0.5) < SUPPORT // 2
    shift = shift - frac
    value = 0.6 * jnp.exp(shift * shift * (-1.0 / 4.5))
    return jnp.where(inside, value, 0.0)


def kernel(
    nx, ny, rp, rq, tx_hbm, ty_hbm, back_hbm, f_hbm, counts_hbm, cells_hbm, fracs_hbm, out_ref,
    tx, ty, back, f, counts, cells, fracs, m2, z, r1, t, r2, wu, wv,
    fsem, lsem, s1, v1, s2, v2,
):
    me_x = lax.axis_index("fx")
    me_y = lax.axis_index("fy")
    rows = f.shape[0]
    cols = f.shape[1]
    step = rows // 4

    small = [
        pltpu.make_async_copy(src, dst, lsem.at[i])
        for i, (src, dst) in enumerate(
            [
                (tx_hbm, tx), (ty_hbm, ty), (cells_hbm, cells), (fracs_hbm, fracs),
                (counts_hbm, counts), (back_hbm, back),
            ]
        )
    ]
    big = [
        pltpu.make_async_copy(
            f_hbm.at[pl.ds(i * step, step)], f.at[pl.ds(i * step, step)], fsem.at[i]
        )
        for i in range(4)
    ]
    with jax.named_scope("a_start"):
        small[0].start()
        big[0].start()
        small[1].start()
        for copy in big[1:] + small[2:]:
            copy.start()

        barrier = pltpu.get_barrier_semaphore()
        for d in range(1, nx):
            pl.semaphore_signal(
                barrier, inc=1, device_id=(lax.rem(me_x + d, nx), me_y), device_id_type=MESH
            )
        for d in range(1, ny):
            pl.semaphore_signal(
                barrier, inc=1, device_id=(me_x, lax.rem(me_y + d, ny)), device_id_type=MESH
            )

    with jax.named_scope("b_c1"):
        small[0].wait()
        wx = tx[pl.ds(2 * nx + rp + me_x, 1), :]
        phi = tx[pl.ds(2 * nx, rp), :] * wx
        c1 = None
        for i in range(4):
            lanes = slice(i * step, (i + 1) * step)
            part = jnp.concatenate(
                [
                    jnp.broadcast_to(tx[pl.ds(r, 1), lanes], (rp, step)) * phi[:, lanes]
                    for r in range(2 * nx)
                ],
                axis=0,
            )
            big[i].wait()
            prod = mm3(split(part), split(f[pl.ds(i * step, step), :]), NN)
            c1 = prod if c1 is None else c1 + prod

    with jax.named_scope("c_d"):
        small[1].wait()
        wy = ty[pl.ds(2 * ny + rq + me_y, 1), :]
        phi = ty[pl.ds(2 * ny, rq), :] * wy
        for r in range(2 * ny):
            m2[pl.ds(r * rq, rq), :] = jnp.broadcast_to(ty[pl.ds(r, 1), :], (rq, cols)) * phi
        prod = mm3(split(c1), split(m2[...]), NT)
        hx = nx * rp
        hy = ny * rq
        z[0] = (prod[:hx, :hy] - prod[hx:, hy:]).reshape(nx, rp, hy)
        z[1] = (prod[:hx, hy:] + prod[hx:, :hy]).reshape(nx, rp, hy)

    with jax.named_scope("d_barrier"):
        pl.semaphore_wait(barrier, nx + ny - 2)
    first = []
    for d in FARX:
        peer = shift_x(me_x, d)
        copy = pltpu.make_async_remote_copy(
            src_ref=z.at[:, peer], dst_ref=r1.at[:, me_x], send_sem=s1.at[d], recv_sem=v1.at[d],
            device_id=(peer, me_y), device_id_type=MESH,
        )
        copy.start()
        first.append(copy)
    r1[:, pl.ds(me_x, 1)] = z[:, pl.ds(me_x, 1)]

    nvis = cells.shape[3]
    wide = WIDE
    kx = 2 * hx
    ky = 2 * hy

    def fill_u(j, carry):
        at = pl.ds(pl.multiple_of(j * wide, wide), wide)
        w = split(weights(cells[0, 0, :, at], fracs[0, 0, :, at], (SUB, wide)))
        high, low = split(mm3((back[:kx, :SUB], back[:kx, SUB:]), w, NN))
        wu[0, :, at] = high
        wu[1, :, at] = low
        return carry

    def fill_v(j, carry):
        at = pl.ds(pl.multiple_of(j * wide, wide), wide)
        w = split(weights(cells[1, 0, :, at], fracs[1, 0, :, at], (SUB, wide)))
        wv[:, at] = mm3((back[kx:, :SUB], back[kx:, SUB:]), w, NN)
        return carry

    with jax.named_scope("f_fillu"):
        for copy in small[2:]:
            copy.wait()
        lax.fori_loop(0, nvis // wide, fill_u, 0)

    with jax.named_scope("g_wait1"):
        for copy in first:
            copy.wait()
    with jax.named_scope("h_tr_send2"):
        for c in range(2):
            t[:, :, c * hx : (c + 1) * hx] = r1[c].reshape(hx, hy).T.reshape(ny, rq, hx)
    second = []
    for d in FARY:
        peer = shift_y(me_y, d)
        copy = pltpu.make_async_remote_copy(
            src_ref=t.at[peer], dst_ref=r2.at[me_y], send_sem=s2.at[d], recv_sem=v2.at[d],
            device_id=(me_x, peer), device_id_type=MESH,
        )
        copy.start()
        second.append(copy)
    r2[pl.ds(me_y, 1)] = t[pl.ds(me_y, 1)]

    with jax.named_scope("i_fillv"):
        lax.fori_loop(0, nvis // wide, fill_v, 0)
    with jax.named_scope("j_wait2"):
        for copy in second:
            copy.wait()

    with jax.named_scope("k_g"):
        got = r2[...].reshape(hy, kx)
        g_re = got[:, :hx]
        g_im = got[:, hx:]
        g = split(
            jnp.concatenate(
                [jnp.concatenate([g_re, -g_im], axis=1), jnp.concatenate([g_im, g_re], axis=1)],
                axis=0,
            )
        )
        live = counts[...]

    def degrid(j, carry):
        at = pl.ds(pl.multiple_of(j * wide, wide), wide)
        sums = mm3(g, (wu[0, :, at], wu[1, :, at]), NN)
        s_re, s_im = sums[:hy], sums[hy:]
        w_re, w_im = wv[:hy, at], wv[hy:, at]
        block = (lax.broadcasted_iota(jnp.int32, (1, wide), 1) + j * wide) // VBLOCK
        alive = block < live
        re = jnp.sum(s_re * w_re - s_im * w_im, axis=0, keepdims=True)
        im = jnp.sum(s_re * w_im + s_im * w_re, axis=0, keepdims=True)
        out_ref[0, 0, :, at] = jnp.where(alive, re, 0.0)
        out_ref[1, 0, :, at] = jnp.where(alive, im, 0.0)
        return carry

    with jax.named_scope("l_degrid"):
        lax.fori_loop(0, nvis // wide, degrid, 0, unroll=UNROLL)


def solution(mesh):
    nx = mesh.shape["fx"]
    ny = mesh.shape["fy"]
    rp, rq = 16, 8

    def per_device(facets, counts, cells, fracs):
        rows, cols = facets.shape
        nvis = cells.shape[3]
        turn_x, right_x, win_x, back_x = axis_tables(nx, rows, nx, rp)
        turn_y, right_y, win_y, back_y = axis_tables(ny, cols, ny, rq)
        tx = jnp.asarray(np.concatenate([turn_x, right_x, win_x]), F32)
        ty = jnp.asarray(np.concatenate([turn_y, right_y, win_y]), F32)
        back = np.concatenate([back_x.real, back_x.imag, back_y.real, back_y.imag], axis=1)
        back = np.ascontiguousarray(back.T).astype(np.float32)
        high = back.astype(BF)
        low = (back - high.astype(np.float32)).astype(BF)
        back = jnp.asarray(np.concatenate([high, low], axis=1))
        hx, hy = nx * rp, ny * rq
        any_spec = pl.BlockSpec(memory_space=pltpu.HBM)
        dma = pltpu.SemaphoreType.DMA
        return pl.pallas_call(
            functools.partial(kernel, nx, ny, rp, rq),
            out_shape=pltpu.VMEM((2, 1, 1, nvis), F32),
            in_specs=[any_spec] * 7,
            out_specs=pl.BlockSpec(memory_space=pltpu.VMEM),
            scratch_shapes=[
                pltpu.VMEM(tx.shape, F32),
                pltpu.VMEM(ty.shape, F32),
                pltpu.VMEM(back.shape, BF),
                pltpu.VMEM((rows, cols), F32),
                pltpu.VMEM((1, 1), jnp.int32),
                pltpu.VMEM(cells.shape, jnp.int32),
                pltpu.VMEM(fracs.shape, F32),
                pltpu.VMEM((2 * hy, cols), F32),
                pltpu.VMEM((2, nx, rp, hy), F32),
                pltpu.VMEM((2, nx, rp, hy), F32),
                pltpu.VMEM((ny, rq, 2 * hx), F32),
                pltpu.VMEM((ny, rq, 2 * hx), F32),
                pltpu.VMEM((2, 2 * hx, nvis), BF),
                pltpu.VMEM((2 * hy, nvis), F32),
                dma((4,)),
                dma((6,)),
                dma((nx,)),
                dma((nx,)),
                dma((ny,)),
                dma((ny,)),
            ],
            compiler_params=pltpu.CompilerParams(
                collective_id=0, has_side_effects=True
            ),
        )(tx, ty, back, facets, counts, cells, fracs)

    spec = P(None, "fx", "fy", None)
    return jax.shard_map(
        per_device,
        mesh=mesh,
        in_specs=(P("fx", "fy"), P("fx", "fy"), spec, spec),
        out_specs=spec,
        check_vma=False,
    )
```

```python
import functools
import math

import jax
import jax.numpy as jnp
import numpy as np
from jax import lax
from jax.experimental import pallas as pl
from jax.experimental.pallas import tpu as pltpu
from jax.sharding import PartitionSpec as P

NIMG = 65536
FP = 4096
SUB = 256
SUPPORT = 8
VBLOCK = 128
LOGICAL = pl.DeviceIdType.LOGICAL
BF = jnp.bfloat16
F32 = jnp.float32


def separable(cells, pixels, rank):
    a = np.arange(cells) - (cells - 1) / 2
    b = np.arange(pixels) - (pixels - 1) / 2
    theta = 2 * np.pi * np.outer(a, b) / NIMG
    half = rank // 2
    uc, sc, vc = np.linalg.svd(np.cos(theta), full_matrices=False)
    us, ss, vs = np.linalg.svd(np.sin(theta), full_matrices=False)
    left = np.concatenate([uc[:, :half] * sc[:half], -1j * us[:, :half] * ss[:half]], axis=1)
    right = np.concatenate([vc[:half], vs[:half]], axis=0)
    norm = math.sqrt(pixels)
    return left / norm, right * norm


def axis_tables(parts, pixels, subs, rank):
    left, right = separable(SUB, pixels, rank)
    right = right * math.sqrt(2.0 / (parts * pixels))
    xx = np.arange(pixels)
    mid = SUB * np.arange(subs) + (SUB - 1) / 2
    phase = 2 * np.pi * ((mid[:, None] * xx[None, :]) / NIMG)
    turn = np.concatenate([np.cos(phase), -np.sin(phase)], axis=0)
    x = np.arange(parts * pixels)
    window = np.sin(np.pi * ((x % FP) + 0.5) / FP).reshape(parts, pixels)
    kk = np.arange(SUB)
    at = (kk[:, None] * np.arange(parts)[None, :] * pixels % NIMG) / NIMG
    at = at + ((kk - (SUB - 1) / 2) * ((pixels - 1) / 2) / NIMG)[:, None]
    back = np.exp(-2j * np.pi * at)[:, :, None] * left[:, None, :]
    return turn, right, window, back.reshape(SUB, parts * rank)


def split(x):
    high = x.astype(BF)
    return high, (x - high.astype(F32)).astype(BF)


def mm(a, b, dims):
    return lax.dot_general(a, b, (dims, ((), ())), preferred_element_type=F32)


def mm3(a, b, dims):
    (ah, al), (bh, bl) = a, b
    return mm(ah, bh, dims) + (mm(ah, bl, dims) + mm(al, bh, dims))


NN = ((1,), (0,))
NT = ((1,), (1,))

WIDE = 512
PEERS = sorted(
    ((a, b) for a in range(8) for b in range(16) if a or b),
    key=lambda o: -(
        2 * (o[0] // 4) + (0, 1, 2, 1)[o[0] % 4] + (0, 1, 2, 1)[o[1] // 4] + (o[1] // 2) % 2
    ),
)


def swap_blocks(x, size):
    shape = (x.shape[0], 8, x.shape[2])
    lane = lax.broadcasted_iota(jnp.int32, shape, 2) // size
    row = lax.broadcasted_iota(jnp.int32, shape, 1)
    width = x.shape[2]
    top, low = x[:, :8], x[:, 8:]
    left = lane < 8
    halves = [
        jnp.where(left, top, pltpu.roll(low, width // 2, 2)),
        jnp.where(left, pltpu.roll(top, width // 2, 2), low),
    ]
    for d in (4, 2, 1):
        up = (row // d) % 2
        same = up == (lane // d) % 2
        for h in range(2):
            v = halves[h]
            right = pltpu.roll(pltpu.roll(v, 8 - d, 1), size * d, 2)
            back = pltpu.roll(pltpu.roll(v, d, 1), width - size * d, 2)
            halves[h] = jnp.where(same, v, jnp.where(up == 0, right, back))
    return jnp.concatenate(halves, axis=1)


def weights(offset, frac, shape):
    cell = lax.broadcasted_iota(jnp.int32, shape, 0).astype(F32)
    shift = cell - (offset.astype(F32) + (SUPPORT // 2 - 1))
    inside = jnp.abs(shift - 0.5) < SUPPORT // 2
    shift = shift - frac
    value = 0.6 * jnp.exp(shift * shift * (-1.0 / 4.5))
    return jnp.where(inside, value, 0.0)


def kernel(
    nx, ny, rp, rq, tx_hbm, ty_hbm, back_hbm, f_hbm, counts_hbm, cells_hbm, fracs_hbm, out_ref,
    tx, ty, back, f, counts, cells, fracs, m2, z, got, wv, wu,
    fsem, lsem, sent, came,
):
    me_x = lax.axis_index("fx")
    me_y = lax.axis_index("fy")
    rows = f.shape[0]
    cols = f.shape[1]
    step = rows // 4

    small = [
        pltpu.make_async_copy(src, dst, lsem.at[i])
        for i, (src, dst) in enumerate(
            [
                (tx_hbm, tx), (ty_hbm, ty), (cells_hbm, cells), (fracs_hbm, fracs),
                (counts_hbm, counts), (back_hbm, back),
            ]
        )
    ]
    big = [
        pltpu.make_async_copy(
            f_hbm.at[pl.ds(i * step, step)], f.at[pl.ds(i * step, step)], fsem.at[i]
        )
        for i in range(4)
    ]
    with jax.named_scope("a_start"):
        small[0].start()
        big[0].start()
        small[1].start()
        for copy in big[1:] + small[2:]:
            copy.start()

        at_x = [((me_x // 4 + a // 4) % 2 * 4 + (me_x + a) % 4) * ny for a in range(nx)]
        at_y = [
            (me_y // 4 + b // 4) % 4 * 4 + (me_y // 2 + b // 2) % 2 * 2 + (me_y + b) % 2
            for b in range(ny)
        ]
        barrier = pltpu.get_barrier_semaphore()
        for a, b in PEERS:
            pl.semaphore_signal(
                barrier, inc=1, device_id=at_x[a] + at_y[b], device_id_type=LOGICAL
            )

    with jax.named_scope("b_c1"):
        small[0].wait()
        wx = tx[pl.ds(2 * nx + rp + me_x, 1), :]
        phi = tx[pl.ds(2 * nx, rp), :] * wx
        c1 = None
        for i in range(4):
            lanes = slice(i * step, (i + 1) * step)
            part = jnp.concatenate(
                [
                    jnp.broadcast_to(tx[pl.ds(r, 1), lanes], (rp, step)) * phi[:, lanes]
                    for r in range(2 * nx)
                ],
                axis=0,
            )
            big[i].wait()
            prod = mm3(split(part), split(f[pl.ds(i * step, step), :]), NN)
            c1 = prod if c1 is None else c1 + prod

    with jax.named_scope("c_d"):
        small[1].wait()
        wy = ty[pl.ds(2 * ny + rq + me_y, 1), :]
        phi = ty[pl.ds(2 * ny, rq), :] * wy
        for r in range(2 * ny):
            m2[pl.ds(r * rq, rq), :] = jnp.broadcast_to(ty[pl.ds(r, 1), :], (rq, cols)) * phi
        prod = mm3(split(c1), split(m2[...]), NT)
        hx = nx * rp
        hy = ny * rq
        re = prod[:hx, :hy] - prod[hx:, hy:]
        im = prod[:hx, hy:] + prod[hx:, :hy]
        both = swap_blocks(jnp.concatenate([re, im]).reshape(2 * nx, rp, hy), rq)
        z[:, 0, :] = both[:nx].reshape(nx * ny, hy)
        z[:, 1, :] = both[nx:].reshape(nx * ny, hy)

    with jax.named_scope("d_barrier"):
        pl.semaphore_wait(barrier, nx * ny - 1)
    with jax.named_scope("e_send"):
        me = me_x * ny + me_y
        for a, b in PEERS:
            peer = at_x[a] + at_y[b]
            pltpu.make_async_remote_copy(
                src_ref=z.at[peer], dst_ref=got.at[me], send_sem=sent, recv_sem=came,
                device_id=peer, device_id_type=LOGICAL,
            ).start()
        got[pl.ds(me, 1)] = z[pl.ds(me, 1)]

    nvis = cells.shape[3]
    wide = WIDE
    kx = 2 * hx
    ky = 2 * hy

    def fill_v(j, carry):
        at = pl.ds(pl.multiple_of(j * wide, wide), wide)
        w = split(weights(cells[1, 0, :, at], fracs[1, 0, :, at], (SUB, wide)))
        high, low = split(mm3((back[kx:, :SUB], back[kx:, SUB:]), w, NN))
        wv[0, :, at] = high
        wv[1, :, at] = low
        return carry

    def fill_u(j, carry):
        at = pl.ds(pl.multiple_of(j * wide, wide), wide)
        w = split(weights(cells[0, 0, :, at], fracs[0, 0, :, at], (SUB, wide)))
        wu[:, at] = mm3((back[:kx, :SUB], back[:kx, SUB:]), w, NN)
        return carry

    with jax.named_scope("f_fill"):
        for copy in small[2:]:
            copy.wait()
        lax.fori_loop(0, nvis // wide, fill_v, 0)
        lax.fori_loop(0, nvis // wide, fill_u, 0)

    with jax.named_scope("g_wait"):
        others = pl.ds(0, nx * ny - 1)
        every = pltpu.make_async_remote_copy(
            src_ref=z.at[others], dst_ref=got.at[others], send_sem=sent, recv_sem=came,
            device_id=me, device_id_type=LOGICAL,
        )
        every.wait()

    with jax.named_scope("k_g"):
        g_re = swap_blocks(got[:, 0, :].reshape(nx, ny, hy), rq).reshape(hx, hy)
        g_im = swap_blocks(got[:, 1, :].reshape(nx, ny, hy), rq).reshape(hx, hy)
        g = split(
            jnp.concatenate(
                [jnp.concatenate([g_re, -g_im], axis=1), jnp.concatenate([g_im, g_re], axis=1)],
                axis=0,
            )
        )
        live = counts[...]

    def degrid(j, carry):
        at = pl.ds(pl.multiple_of(j * wide, wide), wide)
        sums = mm3(g, (wv[0, :, at], wv[1, :, at]), NN)
        s_re, s_im = sums[:hx], sums[hx:]
        w_re, w_im = wu[:hx, at], wu[hx:, at]
        block = (lax.broadcasted_iota(jnp.int32, (1, wide), 1) + j * wide) // VBLOCK
        alive = block < live
        re = jnp.sum(s_re * w_re - s_im * w_im, axis=0, keepdims=True)
        im = jnp.sum(s_re * w_im + s_im * w_re, axis=0, keepdims=True)
        out_ref[0, 0, :, at] = jnp.where(alive, re, 0.0)
        out_ref[1, 0, :, at] = jnp.where(alive, im, 0.0)
        return carry

    with jax.named_scope("l_degrid"):
        lax.fori_loop(0, nvis // wide, degrid, 0, unroll=4)


def solution(mesh):
    nx = mesh.shape["fx"]
    ny = mesh.shape["fy"]
    rp, rq = 16, 8

    def per_device(facets, counts, cells, fracs):
        rows, cols = facets.shape
        nvis = cells.shape[3]
        turn_x, right_x, win_x, back_x = axis_tables(nx, rows, nx, rp)
        turn_y, right_y, win_y, back_y = axis_tables(ny, cols, ny, rq)
        tx = jnp.asarray(np.concatenate([turn_x, right_x, win_x]), F32)
        ty = jnp.asarray(np.concatenate([turn_y, right_y, win_y]), F32)
        back = np.concatenate([back_x.real, back_x.imag, back_y.real, back_y.imag], axis=1)
        back = np.ascontiguousarray(back.T).astype(np.float32)
        high = back.astype(BF)
        low = (back - high.astype(np.float32)).astype(BF)
        back = jnp.asarray(np.concatenate([high, low], axis=1))
        hx, hy = nx * rp, ny * rq
        any_spec = pl.BlockSpec(memory_space=pltpu.HBM)
        dma = pltpu.SemaphoreType.DMA
        return pl.pallas_call(
            functools.partial(kernel, nx, ny, rp, rq),
            out_shape=pltpu.VMEM((2, 1, 1, nvis), F32),
            in_specs=[any_spec] * 7,
            out_specs=pl.BlockSpec(memory_space=pltpu.VMEM),
            scratch_shapes=[
                pltpu.VMEM(tx.shape, F32),
                pltpu.VMEM(ty.shape, F32),
                pltpu.VMEM(back.shape, BF),
                pltpu.VMEM((rows, cols), F32),
                pltpu.VMEM((1, 1), jnp.int32),
                pltpu.VMEM(cells.shape, jnp.int32),
                pltpu.VMEM(fracs.shape, F32),
                pltpu.VMEM((2 * hy, cols), F32),
                pltpu.VMEM((nx * ny, 2, hy), F32),
                pltpu.VMEM((nx * ny, 2, hy), F32),
                pltpu.VMEM((2, 2 * hy, nvis), BF),
                pltpu.VMEM((2 * hx, nvis), F32),
                dma((4,)),
                dma((6,)),
                dma,
                dma,
            ],
            compiler_params=pltpu.CompilerParams(
                collective_id=0, has_side_effects=True
            ),
        )(tx, ty, back, facets, counts, cells, fracs)

    spec = P(None, "fx", "fy", None)
    return jax.shard_map(
        per_device,
        mesh=mesh,
        in_specs=(P("fx", "fy"), P("fx", "fy"), spec, spec),
        out_specs=spec,
        check_vma=False,
    )
```

```python
import functools
import math

import jax
import jax.numpy as jnp
import numpy as np
from jax import lax
from jax.experimental import pallas as pl
from jax.experimental.pallas import tpu as pltpu
from jax.sharding import PartitionSpec as P

NIMG = 65536
FP = 4096
SUB = 256
SUPPORT = 8
VBLOCK = 128
LOGICAL = pl.DeviceIdType.LOGICAL
BF = jnp.bfloat16
F32 = jnp.float32


def separable(cells, pixels, rank):
    a = np.arange(cells) - (cells - 1) / 2
    b = np.arange(pixels) - (pixels - 1) / 2
    theta = 2 * np.pi * np.outer(a, b) / NIMG
    half = rank // 2
    uc, sc, vc = np.linalg.svd(np.cos(theta), full_matrices=False)
    us, ss, vs = np.linalg.svd(np.sin(theta), full_matrices=False)
    left = np.concatenate([uc[:, :half] * sc[:half], -1j * us[:, :half] * ss[:half]], axis=1)
    right = np.concatenate([vc[:half], vs[:half]], axis=0)
    norm = math.sqrt(pixels)
    return left / norm, right * norm


def axis_tables(parts, pixels, subs, rank):
    left, right = separable(SUB, pixels, rank)
    right = right * math.sqrt(2.0 / (parts * pixels))
    xx = np.arange(pixels)
    mid = SUB * np.arange(subs) + (SUB - 1) / 2
    phase = 2 * np.pi * ((mid[:, None] * xx[None, :]) / NIMG)
    turn = np.concatenate([np.cos(phase), -np.sin(phase)], axis=0)
    x = np.arange(parts * pixels)
    window = np.sin(np.pi * ((x % FP) + 0.5) / FP).reshape(parts, pixels)
    kk = np.arange(SUB)
    at = (kk[:, None] * np.arange(parts)[None, :] * pixels % NIMG) / NIMG
    at = at + ((kk - (SUB - 1) / 2) * ((pixels - 1) / 2) / NIMG)[:, None]
    back = np.exp(-2j * np.pi * at)[:, :, None] * left[:, None, :]
    return turn, right, window, back.reshape(SUB, parts * rank)


def split(x):
    high = x.astype(BF)
    return high, (x - high.astype(F32)).astype(BF)


def halves(table, axis):
    table = table.astype(np.float32)
    high = table.astype(BF)
    low = (table - high.astype(np.float32)).astype(BF)
    return jnp.asarray(np.concatenate([high, low], axis=axis))


def mm(a, b, dims):
    return lax.dot_general(a, b, (dims, ((), ())), preferred_element_type=F32)


def mm3(a, b, dims):
    (ah, al), (bh, bl) = a, b
    return mm(ah, bh, dims) + (mm(ah, bl, dims) + mm(al, bh, dims))


NN = ((1,), (0,))
NT = ((1,), (1,))

WIDE = 512
RANK_X = 88
RANK_Y = 48


def place(k):
    return (k // 4 % 4, k // 64 * 2 + k // 2 % 2, k // 16 % 4, k % 2)


def hops(k):
    x, y, z, _ = place(k)
    return sum(min(c, 4 - c) for c in (x, y, z))


def launch_order(k):
    x, y, z, core = place(k)
    return ((z * 4 + y) * 4 + x, 1 - core)


SENDS = sorted(range(128), key=launch_order)
SIGNALS = sorted(range(128), key=lambda k: (-hops(k), launch_order(k)))


def compress(back, rank):
    terms = back.shape[1]
    u, s, v = np.linalg.svd(np.concatenate([back.real, back.imag], axis=1), full_matrices=False)
    rest = s[:rank, None] * v[:rank]
    return u[:, :rank], rest[:, :terms], rest[:, terms:]


def swap_blocks(parts, size):
    parts = list(parts)
    width = parts[0].shape[1]
    lane = lax.broadcasted_iota(jnp.int32, parts[0].shape, 1) // size
    d = len(parts) // 2
    while d:
        low = (lane // d) % 2 == 0
        for p in range(len(parts)):
            if p // d % 2 == 0:
                a, b = parts[p], parts[p + d]
                parts[p] = jnp.where(low, a, pltpu.roll(b, size * d, 1))
                parts[p + d] = jnp.where(low, pltpu.roll(a, width - size * d, 1), b)
        d //= 2
    return parts


def weights(offset, frac, shape):
    cell = lax.broadcasted_iota(jnp.int32, shape, 0).astype(F32)
    shift = cell - (offset.astype(F32) + (SUPPORT // 2 - 1))
    inside = jnp.abs(shift - 0.5) < SUPPORT // 2
    shift = shift - frac
    value = 0.6 * jnp.exp(shift * shift * (-1.0 / 4.5))
    return jnp.where(inside, value, 0.0)


def kernel(
    nx, ny, rp, rq, tx_hbm, ty_hbm, cell_hbm, rx_hbm, ry_hbm, f_hbm, counts_hbm, cells_hbm, fracs_hbm, out_ref,
    tx, ty, cell, rx, ry, f, counts, cells, fracs, m2, z, got, wv, wu,
    fsem, lsem, sent, came,
):
    me_x = lax.axis_index("fx")
    me_y = lax.axis_index("fy")
    rows = f.shape[0]
    cols = f.shape[1]
    step = rows // 4

    small = [
        pltpu.make_async_copy(src, dst, lsem.at[i])
        for i, (src, dst) in enumerate(
            [
                (tx_hbm, tx), (ty_hbm, ty), (cells_hbm, cells), (fracs_hbm, fracs),
                (counts_hbm, counts), (cell_hbm, cell), (rx_hbm, rx), (ry_hbm, ry),
            ]
        )
    ]
    big = [
        pltpu.make_async_copy(
            f_hbm.at[pl.ds(i * step, step)], f.at[pl.ds(i * step, step)], fsem.at[i]
        )
        for i in range(4)
    ]
    with jax.named_scope("a_start"):
        small[0].start()
        big[0].start()
        small[1].start()
        for copy in big[1:] + small[2:]:
            copy.start()

        barrier = pltpu.get_barrier_semaphore()
        me = me_x * ny + me_y
        for k in SIGNALS:

            @pl.when(me != k)
            def _():
                pl.semaphore_signal(barrier, inc=1, device_id=k, device_id_type=LOGICAL)

    with jax.named_scope("b_c1"):
        small[0].wait()
        wx = tx[pl.ds(2 * nx + rp + me_x, 1), :]
        phi = tx[pl.ds(2 * nx, rp), :] * wx
        c1 = None
        for i in range(4):
            lanes = slice(i * step, (i + 1) * step)
            part = jnp.concatenate(
                [
                    tx[c * nx : (c + 1) * nx, lanes] * phi[p : p + 1, lanes]
                    for c in range(2)
                    for p in range(rp)
                ],
                axis=0,
            )
            big[i].wait()
            prod = mm3(split(part), split(f[pl.ds(i * step, step), :]), NN)
            c1 = prod if c1 is None else c1 + prod

    with jax.named_scope("c_d"):
        small[1].wait()
        wy = ty[pl.ds(2 * ny + rq + me_y, 1), :]
        phi = ty[pl.ds(2 * ny, rq), :] * wy
        for r in range(2 * ny):
            m2[pl.ds(r * rq, rq), :] = jnp.broadcast_to(ty[pl.ds(r, 1), :], (rq, cols)) * phi
        prod = mm3(split(c1), split(m2[...]), NT)
        hx = nx * rp
        hy = ny * rq
        re = prod[:hx, :hy] - prod[hx:, hy:]
        im = prod[:hx, hy:] + prod[hx:, :hy]
        for c, part in enumerate((re, im)):
            swapped = swap_blocks([part[p * nx : (p + 1) * nx] for p in range(rp)], rq)
            for v in range(ny):
                z[v * nx : (v + 1) * nx, c, :] = swapped[v]

    nvis = cells.shape[3]
    wide = WIDE
    kx = rx.shape[0] // 2
    ky = cell.shape[0] - kx

    def fill_v(j, carry):
        at = pl.ds(pl.multiple_of(j * wide, wide), wide)
        w = split(weights(cells[1, 0, :, at], fracs[1, 0, :, at], (SUB, wide)))
        high, low = split(mm3((cell[kx:, :SUB], cell[kx:, SUB:]), w, NN))
        wv[:ky, at] = high
        wv[ky : 2 * ky, at] = high
        wv[2 * ky :, at] = low
        return carry

    def fill_u(j, carry):
        at = pl.ds(pl.multiple_of(j * wide, wide), wide)
        w = split(weights(cells[0, 0, :, at], fracs[0, 0, :, at], (SUB, wide)))
        wu[:, at] = mm3((cell[:kx, :SUB], cell[:kx, SUB:]), w, NN)
        return carry

    chunks = nvis // wide
    early = lax.div(3 - lax.rem(me_x, 4), 3) * chunks
    with jax.named_scope("c_fill"):
        for copy in small[2:]:
            copy.wait()
        lax.fori_loop(0, early, fill_v, 0)

    with jax.named_scope("d_barrier"):
        pl.semaphore_wait(barrier, nx * ny - 1)
    with jax.named_scope("e_send"):
        slot = me_y * nx + me_x
        for k in SENDS:

            @pl.when(me != k)
            def _():
                pltpu.make_async_remote_copy(
                    src_ref=z.at[k % ny * nx + k // ny], dst_ref=got.at[slot],
                    send_sem=sent, recv_sem=came, device_id=k, device_id_type=LOGICAL,
                ).start()

        got[pl.ds(slot, 1)] = z[pl.ds(slot, 1)]

    with jax.named_scope("f_fill"):
        lax.fori_loop(early, chunks, fill_v, 0)
        lax.fori_loop(0, chunks, fill_u, 0)

    with jax.named_scope("g_wait"):
        others = pl.ds(0, nx * ny - 1)
        every = pltpu.make_async_remote_copy(
            src_ref=z.at[others], dst_ref=got.at[others], send_sem=sent, recv_sem=came,
            device_id=me, device_id_type=LOGICAL,
        )
        every.wait()

    with jax.named_scope("k_g"):
        g_re, g_im = (
            jnp.concatenate(
                swap_blocks([got[v * nx : (v + 1) * nx, c, :] for v in range(ny)], rq)
            )
            for c in range(2)
        )
        g = split(
            jnp.concatenate(
                [jnp.concatenate([g_re, -g_im], axis=1), jnp.concatenate([g_im, g_re], axis=1)],
                axis=0,
            )
        )
        g = split(mm3(g, (ry[0], ry[1]), NN))
        g = mm3((rx[:, : 2 * hx], rx[:, 2 * hx :]), g, NN)
        high, low = split(g)
        copy_of = lax.broadcasted_iota(jnp.int32, g.shape, 1) // ky
        g = jnp.where(copy_of == 1, low.astype(F32), high.astype(F32)).astype(BF)
        live = counts[...]

    def degrid(j, carry):
        at = pl.ds(pl.multiple_of(j * wide, wide), wide)
        sums = mm(g, wv[:, at], NN)
        w = wu[:, at]
        block = (lax.broadcasted_iota(jnp.int32, (1, wide), 1) + j * wide) // VBLOCK
        alive = block < live
        re = jnp.sum(sums[:kx] * w, axis=0, keepdims=True)
        im = jnp.sum(sums[kx:] * w, axis=0, keepdims=True)
        out_ref[0, 0, :, at] = jnp.where(alive, re, 0.0)
        out_ref[1, 0, :, at] = jnp.where(alive, im, 0.0)
        return carry

    with jax.named_scope("l_degrid"):
        lax.fori_loop(0, nvis // wide, degrid, 0, unroll=4)


def solution(mesh):
    nx = mesh.shape["fx"]
    ny = mesh.shape["fy"]
    rp, rq = 16, 8

    def per_device(facets, counts, cells, fracs):
        rows, cols = facets.shape
        nvis = cells.shape[3]
        turn_x, right_x, win_x, back_x = axis_tables(nx, rows, nx, rp)
        turn_y, right_y, win_y, back_y = axis_tables(ny, cols, ny, rq)
        tx = jnp.asarray(np.concatenate([turn_x, right_x, win_x]), F32)
        ty = jnp.asarray(np.concatenate([turn_y, right_y, win_y]), F32)
        back_x = back_x.reshape(SUB, nx, rp).swapaxes(1, 2).reshape(SUB, nx * rp)
        base_x, re_x, im_x = compress(back_x, RANK_X)
        base_y, re_y, im_y = compress(back_y, RANK_Y)
        cell = halves(np.concatenate([base_x.T, base_y.T]), 1)
        rx = halves(
            np.concatenate(
                [np.concatenate([re_x, -im_x], axis=1), np.concatenate([im_x, re_x], axis=1)]
            ),
            1,
        )
        ry = np.concatenate([re_y, im_y], axis=1).T
        ry = halves(np.concatenate([ry, ry, ry], axis=1)[None], 0)
        hx, hy = nx * rp, ny * rq
        any_spec = pl.BlockSpec(memory_space=pltpu.HBM)
        dma = pltpu.SemaphoreType.DMA
        return pl.pallas_call(
            functools.partial(kernel, nx, ny, rp, rq),
            out_shape=pltpu.VMEM((2, 1, 1, nvis), F32),
            in_specs=[any_spec] * 9,
            out_specs=pl.BlockSpec(memory_space=pltpu.VMEM),
            scratch_shapes=[
                pltpu.VMEM(tx.shape, F32),
                pltpu.VMEM(ty.shape, F32),
                pltpu.VMEM(cell.shape, BF),
                pltpu.VMEM(rx.shape, BF),
                pltpu.VMEM(ry.shape, BF),
                pltpu.VMEM((rows, cols), F32),
                pltpu.VMEM((1, 1), jnp.int32),
                pltpu.VMEM(cells.shape, jnp.int32),
                pltpu.VMEM(fracs.shape, F32),
                pltpu.VMEM((2 * hy, cols), F32),
                pltpu.VMEM((nx * ny, 2, hy), F32),
                pltpu.VMEM((nx * ny, 2, hy), F32),
                pltpu.VMEM((3 * RANK_Y, nvis), BF),
                pltpu.VMEM((RANK_X, nvis), F32),
                dma((4,)),
                dma((8,)),
                dma,
                dma,
            ],
            compiler_params=pltpu.CompilerParams(
                collective_id=0, has_side_effects=True
            ),
        )(tx, ty, cell, rx, ry, facets, counts, cells, fracs)

    spec = P(None, "fx", "fy", None)
    return jax.shard_map(
        per_device,
        mesh=mesh,
        in_specs=(P("fx", "fy"), P("fx", "fy"), spec, spec),
        out_specs=spec,
        check_vma=False,
    )
```

```python
import functools
import math

import jax
import jax.numpy as jnp
import numpy as np
from jax import lax
from jax.experimental import pallas as pl
from jax.experimental.pallas import tpu as pltpu
from jax.sharding import PartitionSpec as P

NIMG = 65536
FP = 4096
SUB = 256
SUPPORT = 8
VBLOCK = 128
LOGICAL = pl.DeviceIdType.LOGICAL
BF = jnp.bfloat16
F32 = jnp.float32


def separable(cells, pixels, rank):
    a = np.arange(cells) - (cells - 1) / 2
    b = np.arange(pixels) - (pixels - 1) / 2
    theta = 2 * np.pi * np.outer(a, b) / NIMG
    half = rank // 2
    uc, sc, vc = np.linalg.svd(np.cos(theta), full_matrices=False)
    us, ss, vs = np.linalg.svd(np.sin(theta), full_matrices=False)
    left = np.concatenate([uc[:, :half] * sc[:half], -1j * us[:, :half] * ss[:half]], axis=1)
    right = np.concatenate([vc[:half], vs[:half]], axis=0)
    norm = math.sqrt(pixels)
    return left / norm, right * norm


def axis_tables(parts, pixels, subs, rank):
    left, right = separable(SUB, pixels, rank)
    right = right * math.sqrt(2.0 / (parts * pixels))
    xx = np.arange(pixels)
    mid = SUB * np.arange(subs) + (SUB - 1) / 2
    phase = 2 * np.pi * ((mid[:, None] * xx[None, :]) / NIMG)
    turn = np.concatenate([np.cos(phase), -np.sin(phase)], axis=0)
    x = np.arange(parts * pixels)
    window = np.sin(np.pi * ((x % FP) + 0.5) / FP).reshape(parts, pixels)
    kk = np.arange(SUB)
    at = (kk[:, None] * np.arange(parts)[None, :] * pixels % NIMG) / NIMG
    at = at + ((kk - (SUB - 1) / 2) * ((pixels - 1) / 2) / NIMG)[:, None]
    back = np.exp(-2j * np.pi * at)[:, :, None] * left[:, None, :]
    return turn, right, window, back.reshape(SUB, parts * rank)


def split(x):
    high = x.astype(BF)
    return high, (x - high.astype(F32)).astype(BF)


def halves(table, axis):
    table = table.astype(np.float32)
    high = table.astype(BF)
    low = (table - high.astype(np.float32)).astype(BF)
    return jnp.asarray(np.concatenate([high, low], axis=axis))


def mm(a, b, dims):
    return lax.dot_general(a, b, (dims, ((), ())), preferred_element_type=F32)


def mm3(a, b, dims):
    (ah, al), (bh, bl) = a, b
    return mm(ah, bh, dims) + (mm(ah, bl, dims) + mm(al, bh, dims))


NN = ((1,), (0,))
NT = ((1,), (1,))

WIDE = 512
RANK_X = 80
RANK_Y = 48


def place(k):
    return (k // 4 % 4, k // 64 * 2 + k // 2 % 2, k // 16 % 4, k % 2)


def hops(k):
    x, y, z, _ = place(k)
    return sum(min(c, 4 - c) for c in (x, y, z))


def launch_order(k):
    x, y, z, core = place(k)
    return ((z * 4 + y) * 4 + x, 1 - core)


SENDS = sorted(range(128), key=launch_order)
SIGNALS = sorted(range(128), key=lambda k: (-hops(k), launch_order(k)))


def compress(back, rank):
    terms = back.shape[1]
    u, s, v = np.linalg.svd(np.concatenate([back.real, back.imag], axis=1), full_matrices=False)
    rest = s[:rank, None] * v[:rank]
    return u[:, :rank], rest[:, :terms], rest[:, terms:]


def swap_blocks(parts, size):
    parts = list(parts)
    width = parts[0].shape[1]
    lane = lax.broadcasted_iota(jnp.int32, parts[0].shape, 1) // size
    d = len(parts) // 2
    while d:
        low = (lane // d) % 2 == 0
        for p in range(len(parts)):
            if p // d % 2 == 0:
                a, b = parts[p], parts[p + d]
                parts[p] = jnp.where(low, a, pltpu.roll(b, size * d, 1))
                parts[p + d] = jnp.where(low, pltpu.roll(a, width - size * d, 1), b)
        d //= 2
    return parts


def weights(offset, frac, shape):
    cell = lax.broadcasted_iota(jnp.int32, shape, 0).astype(F32)
    shift = cell - (offset.astype(F32) + (SUPPORT // 2 - 1))
    inside = jnp.abs(shift - 0.5) < SUPPORT // 2
    shift = shift - frac
    value = 0.6 * jnp.exp(shift * shift * (-1.0 / 4.5))
    return jnp.where(inside, value, 0.0)


def kernel(
    nx, ny, rp, rq, tx_hbm, ty_hbm, cell_hbm, rx_hbm, ry_hbm, f_hbm, counts_hbm, cells_hbm, fracs_hbm, out_ref,
    tx, ty, cell, rx, ry, f, counts, cells, fracs, m2, z, got, wu, wv,
    fsem, lsem, sent, came,
):
    me_x = lax.axis_index("fx")
    me_y = lax.axis_index("fy")
    rows = f.shape[0]
    cols = f.shape[1]
    step = rows // 4

    small = [
        pltpu.make_async_copy(src, dst, lsem.at[i])
        for i, (src, dst) in enumerate(
            [
                (tx_hbm, tx), (ty_hbm, ty), (cells_hbm, cells), (fracs_hbm, fracs),
                (counts_hbm, counts), (cell_hbm, cell), (rx_hbm, rx), (ry_hbm, ry),
            ]
        )
    ]
    big = [
        pltpu.make_async_copy(
            f_hbm.at[pl.ds(i * step, step)], f.at[pl.ds(i * step, step)], fsem.at[i]
        )
        for i in range(4)
    ]
    with jax.named_scope("a_start"):
        small[0].start()
        big[0].start()
        small[1].start()
        for copy in big[1:] + small[2:]:
            copy.start()

        barrier = pltpu.get_barrier_semaphore()
        me = me_x * ny + me_y
        for k in SIGNALS:

            @pl.when(me != k)
            def _():
                pl.semaphore_signal(barrier, inc=1, device_id=k, device_id_type=LOGICAL)

    with jax.named_scope("b_c1"):
        small[0].wait()
        wx = tx[pl.ds(2 * nx + rp + me_x, 1), :]
        phi = tx[pl.ds(2 * nx, rp), :] * wx
        c1 = None
        for i in range(4):
            lanes = slice(i * step, (i + 1) * step)
            part = jnp.concatenate(
                [
                    tx[c * nx : (c + 1) * nx, lanes] * phi[p : p + 1, lanes]
                    for c in range(2)
                    for p in range(rp)
                ],
                axis=0,
            )
            big[i].wait()
            prod = mm3(split(part), split(f[pl.ds(i * step, step), :]), NN)
            c1 = prod if c1 is None else c1 + prod

    with jax.named_scope("c_d"):
        small[1].wait()
        wy = ty[pl.ds(2 * ny + rq + me_y, 1), :]
        phi = ty[pl.ds(2 * ny, rq), :] * wy
        for r in range(2 * ny):
            m2[pl.ds(r * rq, rq), :] = jnp.broadcast_to(ty[pl.ds(r, 1), :], (rq, cols)) * phi
        prod = mm3(split(c1), split(m2[...]), NT)
        hx = nx * rp
        hy = ny * rq
        re = prod[:hx, :hy] - prod[hx:, hy:]
        im = prod[:hx, hy:] + prod[hx:, :hy]
        for c, part in enumerate((re, im)):
            swapped = swap_blocks([part[p * nx : (p + 1) * nx] for p in range(rp)], rq)
            for v in range(ny):
                z[v * nx : (v + 1) * nx, c, :] = swapped[v]

    nvis = cells.shape[3]
    wide = WIDE
    kx = RANK_X
    ky = RANK_Y

    def fill_u(j, carry):
        at = pl.ds(pl.multiple_of(j * wide, wide), wide)
        w = split(weights(cells[0, 0, :, at], fracs[0, 0, :, at], (SUB, wide)))
        high, low = split(mm3((cell[:kx, :SUB], cell[:kx, SUB:]), w, NN))
        wu[:kx, at] = high
        wu[kx : 2 * kx, at] = high
        wu[2 * kx :, at] = low
        return carry

    def fill_v(j, carry):
        at = pl.ds(pl.multiple_of(j * wide, wide), wide)
        w = split(weights(cells[1, 0, :, at], fracs[1, 0, :, at], (SUB, wide)))
        wv[:, at] = mm3((cell[kx:, :SUB], cell[kx:, SUB:]), w, NN)
        return carry

    chunks = nvis // wide
    early = lax.div(3 - lax.rem(me_x, 4), 3) * chunks
    with jax.named_scope("c_fill"):
        for copy in small[2:]:
            copy.wait()
        lax.fori_loop(0, early, fill_v, 0)

    with jax.named_scope("d_barrier"):
        pl.semaphore_wait(barrier, nx * ny - 1)
    with jax.named_scope("e_send"):
        slot = me_y * nx + me_x
        for k in SENDS:

            @pl.when(me != k)
            def _():
                pltpu.make_async_remote_copy(
                    src_ref=z.at[k % ny * nx + k // ny], dst_ref=got.at[slot],
                    send_sem=sent, recv_sem=came, device_id=k, device_id_type=LOGICAL,
                ).start()

        got[pl.ds(slot, 1)] = z[pl.ds(slot, 1)]

    with jax.named_scope("f_fill"):
        lax.fori_loop(early, chunks, fill_v, 0)
        lax.fori_loop(0, chunks, fill_u, 0)

    with jax.named_scope("g_wait"):
        others = pl.ds(0, nx * ny - 1)
        every = pltpu.make_async_remote_copy(
            src_ref=z.at[others], dst_ref=got.at[others], send_sem=sent, recv_sem=came,
            device_id=me, device_id_type=LOGICAL,
        )
        every.wait_recv()

    with jax.named_scope("k_swap"):
        sums = split(
            jnp.concatenate(
                [
                    part
                    for c in range(2)
                    for part in swap_blocks(
                        [got[v * nx : (v + 1) * nx, c, :] for v in range(ny)], rq
                    )
                ]
            )
        )
    with jax.named_scope("k_h"):
        both = mm3((ry[:, :hy], ry[:, hy:]), sums, NT)
        h_re = both[:ky, :hx] - both[ky:, hx:]
        h_im = both[:ky, hx:] + both[ky:, :hx]
        h = split(
            jnp.concatenate(
                [jnp.concatenate([h_re, -h_im], axis=1), jnp.concatenate([h_im, h_re], axis=1)],
                axis=0,
            )
        )
    with jax.named_scope("k_g2"):
        g = mm3(h, (rx[0], rx[1]), NN)
        high, low = split(g)
        copy_of = lax.broadcasted_iota(jnp.int32, g.shape, 1) // kx
        g = jnp.where(copy_of == 1, low.astype(F32), high.astype(F32)).astype(BF)
        live = counts[...]

    def degrid(j, carry):
        at = pl.ds(pl.multiple_of(j * wide, wide), wide)
        sums = mm(g, wu[:, at], NN)
        w = wv[:, at]
        block = (lax.broadcasted_iota(jnp.int32, (1, wide), 1) + j * wide) // VBLOCK
        alive = block < live
        re = jnp.sum(sums[:ky] * w, axis=0, keepdims=True)
        im = jnp.sum(sums[ky:] * w, axis=0, keepdims=True)
        out_ref[0, 0, :, at] = jnp.where(alive, re, 0.0)
        out_ref[1, 0, :, at] = jnp.where(alive, im, 0.0)
        return carry

    with jax.named_scope("l_degrid"):
        lax.fori_loop(0, nvis // wide, degrid, 0, unroll=4)
    with jax.named_scope("m_sent"):
        every.wait_send()


def solution(mesh):
    nx = mesh.shape["fx"]
    ny = mesh.shape["fy"]
    rp, rq = 16, 8

    def per_device(facets, counts, cells, fracs):
        rows, cols = facets.shape
        nvis = cells.shape[3]
        turn_x, right_x, win_x, back_x = axis_tables(nx, rows, nx, rp)
        turn_y, right_y, win_y, back_y = axis_tables(ny, cols, ny, rq)
        tx = jnp.asarray(np.concatenate([turn_x, right_x, win_x]), F32)
        ty = jnp.asarray(np.concatenate([turn_y, right_y, win_y]), F32)
        back_x = back_x.reshape(SUB, nx, rp).swapaxes(1, 2).reshape(SUB, nx * rp)
        base_x, re_x, im_x = compress(back_x, RANK_X)
        base_y, re_y, im_y = compress(back_y, RANK_Y)
        cell = halves(np.concatenate([base_x.T, base_y.T]), 1)
        rx = np.concatenate([re_x, im_x], axis=1).T
        rx = halves(np.concatenate([rx, rx, rx], axis=1)[None], 0)
        ry = halves(np.concatenate([re_y, im_y]), 1)
        hx, hy = nx * rp, ny * rq
        any_spec = pl.BlockSpec(memory_space=pltpu.HBM)
        dma = pltpu.SemaphoreType.DMA
        return pl.pallas_call(
            functools.partial(kernel, nx, ny, rp, rq),
            out_shape=pltpu.VMEM((2, 1, 1, nvis), F32),
            in_specs=[any_spec] * 9,
            out_specs=pl.BlockSpec(memory_space=pltpu.VMEM),
            scratch_shapes=[
                pltpu.VMEM(tx.shape, F32),
                pltpu.VMEM(ty.shape, F32),
                pltpu.VMEM(cell.shape, BF),
                pltpu.VMEM(rx.shape, BF),
                pltpu.VMEM(ry.shape, BF),
                pltpu.VMEM((rows, cols), F32),
                pltpu.VMEM((1, 1), jnp.int32),
                pltpu.VMEM(cells.shape, jnp.int32),
                pltpu.VMEM(fracs.shape, F32),
                pltpu.VMEM((2 * hy, cols), F32),
                pltpu.VMEM((nx * ny, 2, hy), F32),
                pltpu.VMEM((nx * ny, 2, hy), F32),
                pltpu.VMEM((3 * RANK_X, nvis), BF),
                pltpu.VMEM((RANK_Y, nvis), F32),
                dma((4,)),
                dma((8,)),
                dma,
                dma,
            ],
            compiler_params=pltpu.CompilerParams(
                collective_id=0, has_side_effects=True
            ),
        )(tx, ty, cell, rx, ry, facets, counts, cells, fracs)

    spec = P(None, "fx", "fy", None)
    return jax.shard_map(
        per_device,
        mesh=mesh,
        in_specs=(P("fx", "fy"), P("fx", "fy"), spec, spec),
        out_specs=spec,
        check_vma=False,
    )
```

```python
import functools
import math

import jax
import jax.numpy as jnp
import numpy as np
from jax import lax
from jax.experimental import pallas as pl
from jax.experimental.pallas import tpu as pltpu
from jax.sharding import PartitionSpec as P

NIMG = 65536
FP = 4096
SUB = 256
SUPPORT = 8
VBLOCK = 128
LOGICAL = pl.DeviceIdType.LOGICAL
BF = jnp.bfloat16
F32 = jnp.float32


def separable(cells, pixels, rank):
    a = np.arange(cells) - (cells - 1) / 2
    b = np.arange(pixels) - (pixels - 1) / 2
    theta = 2 * np.pi * np.outer(a, b) / NIMG
    half = rank // 2
    uc, sc, vc = np.linalg.svd(np.cos(theta), full_matrices=False)
    us, ss, vs = np.linalg.svd(np.sin(theta), full_matrices=False)
    left = np.concatenate([uc[:, :half] * sc[:half], -1j * us[:, :half] * ss[:half]], axis=1)
    right = np.concatenate([vc[:half], vs[:half]], axis=0)
    norm = math.sqrt(pixels)
    return left / norm, right * norm


def axis_tables(parts, pixels, subs, rank):
    left, right = separable(SUB, pixels, rank)
    right = right * math.sqrt(2.0 / (parts * pixels))
    xx = np.arange(pixels)
    mid = SUB * np.arange(subs) + (SUB - 1) / 2
    phase = 2 * np.pi * ((mid[:, None] * xx[None, :]) / NIMG)
    turn = np.concatenate([np.cos(phase), -np.sin(phase)], axis=0)
    x = np.arange(parts * pixels)
    window = np.sin(np.pi * ((x % FP) + 0.5) / FP).reshape(parts, pixels)
    kk = np.arange(SUB)
    at = (kk[:, None] * np.arange(parts)[None, :] * pixels % NIMG) / NIMG
    at = at + ((kk - (SUB - 1) / 2) * ((pixels - 1) / 2) / NIMG)[:, None]
    back = np.exp(-2j * np.pi * at)[:, :, None] * left[:, None, :]
    return turn, right, window, back.reshape(SUB, parts * rank)


def split(x):
    high = x.astype(BF)
    return high, (x - high.astype(F32)).astype(BF)


def halves(table, axis):
    table = table.astype(np.float32)
    high = table.astype(BF)
    low = (table - high.astype(np.float32)).astype(BF)
    return jnp.asarray(np.concatenate([high, low], axis=axis))


def mm(a, b, dims):
    return lax.dot_general(a, b, (dims, ((), ())), preferred_element_type=F32)


def mm3(a, b, dims):
    (ah, al), (bh, bl) = a, b
    return mm(ah, bh, dims) + (mm(ah, bl, dims) + mm(al, bh, dims))


NN = ((1,), (0,))
NT = ((1,), (1,))

WIDE = 512
RANK_X = 80
RANK_Y = 48


def place(k):
    return (k // 4 % 4, k // 64 * 2 + k // 2 % 2, k // 16 % 4, k % 2)


def hops(k):
    x, y, z, _ = place(k)
    return sum(min(c, 4 - c) for c in (x, y, z))


def launch_order(k):
    x, y, z, core = place(k)
    return ((z * 4 + y) * 4 + x, 1 - core)


SENDS = sorted(range(128), key=launch_order)
SIGNALS = sorted(range(128), key=lambda k: (-hops(k), launch_order(k)))


def compress(back, rank):
    terms = back.shape[1]
    u, s, v = np.linalg.svd(np.concatenate([back.real, back.imag], axis=1), full_matrices=False)
    rest = s[:rank, None] * v[:rank]
    return u[:, :rank], rest[:, :terms], rest[:, terms:]


def pick_blocks(parts, size):
    n = len(parts)
    block = lax.broadcasted_iota(jnp.int32, parts[0].shape, 1) // size
    d = 1
    while d < n:
        up = (block // d) % 2 == 1
        parts = [jnp.where(up, parts[(i + d) % n], parts[i]) for i in range(n)]
        d *= 2
    return [parts[-s % n] for s in range(n)]


def rolled(part, shift):
    return part if isinstance(shift, int) and shift == 0 else pltpu.roll(part, shift, 1)


def weights(offset, frac, shape):
    cell = lax.broadcasted_iota(jnp.int32, shape, 0).astype(F32)
    shift = cell - (offset.astype(F32) + (SUPPORT // 2 - 1))
    inside = jnp.abs(shift - 0.5) < SUPPORT // 2
    shift = shift - frac
    value = 0.6 * jnp.exp(shift * shift * (-1.0 / 4.5))
    return jnp.where(inside, value, 0.0)


def kernel(
    nx, ny, rp, rq, tx_hbm, ty_hbm, cell_hbm, rx_hbm, ry_hbm, f_hbm, counts_hbm, cells_hbm, fracs_hbm, out_ref,
    tx, ty, cell, rx, ry, f, counts, cells, fracs, m2, z, got, wu, wv,
    fsem, lsem, sent, came,
):
    me_x = lax.axis_index("fx")
    me_y = lax.axis_index("fy")
    rows = f.shape[0]
    cols = f.shape[1]
    step = rows // 4

    small = [
        pltpu.make_async_copy(src, dst, lsem.at[i])
        for i, (src, dst) in enumerate(
            [
                (tx_hbm, tx), (ty_hbm, ty), (cells_hbm, cells), (fracs_hbm, fracs),
                (counts_hbm, counts), (cell_hbm, cell), (rx_hbm, rx), (ry_hbm, ry),
            ]
        )
    ]
    big = [
        pltpu.make_async_copy(
            f_hbm.at[pl.ds(i * step, step)], f.at[pl.ds(i * step, step)], fsem.at[i]
        )
        for i in range(4)
    ]
    with jax.named_scope("a_start"):
        small[0].start()
        big[0].start()
        small[1].start()
        for copy in big[1:] + small[2:]:
            copy.start()

        barrier = pltpu.get_barrier_semaphore()
        me = me_x * ny + me_y
        for k in SIGNALS:

            @pl.when(me != k)
            def _():
                pl.semaphore_signal(barrier, inc=1, device_id=k, device_id_type=LOGICAL)

    with jax.named_scope("b_c1"):
        small[0].wait()
        wx = tx[pl.ds(2 * nx + rp + me_x, 1), :]
        phi = tx[pl.ds(2 * nx, rp), :] * wx
        c1 = None
        for i in range(4):
            lanes = slice(i * step, (i + 1) * step)
            part = jnp.concatenate(
                [
                    tx[c * nx : (c + 1) * nx, lanes] * phi[p : p + 1, lanes]
                    for c in range(2)
                    for p in range(rp)
                ],
                axis=0,
            )
            big[i].wait()
            prod = mm3(split(part), split(f[pl.ds(i * step, step), :]), NN)
            c1 = prod if c1 is None else c1 + prod

    with jax.named_scope("c_d"):
        small[1].wait()
        wy = ty[pl.ds(2 * ny + rq + me_y, 1), :]
        phi = ty[pl.ds(2 * ny, rq), :] * wy
        for r in range(2 * ny):
            m2[pl.ds(r * rq, rq), :] = jnp.broadcast_to(ty[pl.ds(r, 1), :], (rq, cols)) * phi
        prod = mm3(split(c1), split(m2[...]), NT)
        hx = nx * rp
        hy = ny * rq
        re = prod[:hx, :hy] - prod[hx:, hy:]
        im = prod[:hx, hy:] + prod[hx:, :hy]
        for c, part in enumerate((re, im)):
            swapped = pick_blocks(
                [rolled(part[p * nx : (p + 1) * nx], p * rq) for p in range(rp)], rq
            )
            for v in range(ny):
                turn = lax.rem(me_y + (ny - v), ny) * rq
                z[v * nx : (v + 1) * nx, c, :] = rolled(swapped[v], turn)

    nvis = cells.shape[3]
    wide = WIDE
    kx = RANK_X
    ky = RANK_Y

    def fill_u(j, carry):
        at = pl.ds(pl.multiple_of(j * wide, wide), wide)
        w = split(weights(cells[0, 0, :, at], fracs[0, 0, :, at], (SUB, wide)))
        high, low = split(mm3((cell[:kx, :SUB], cell[:kx, SUB:]), w, NN))
        wu[:kx, at] = high
        wu[kx : 2 * kx, at] = high
        wu[2 * kx :, at] = low
        return carry

    def fill_v(j, carry):
        at = pl.ds(pl.multiple_of(j * wide, wide), wide)
        w = split(weights(cells[1, 0, :, at], fracs[1, 0, :, at], (SUB, wide)))
        wv[:, at] = mm3((cell[kx:, :SUB], cell[kx:, SUB:]), w, NN)
        return carry

    chunks = nvis // wide
    early = lax.div(3 - lax.rem(me_x, 4), 3) * chunks
    with jax.named_scope("c_fill"):
        for copy in small[2:]:
            copy.wait()
        lax.fori_loop(0, early, fill_v, 0)

    with jax.named_scope("d_barrier"):
        pl.semaphore_wait(barrier, nx * ny - 1)
    with jax.named_scope("e_send"):
        slot = me_y * nx + me_x
        for k in SENDS:

            @pl.when(me != k)
            def _():
                pltpu.make_async_remote_copy(
                    src_ref=z.at[k % ny * nx + k // ny], dst_ref=got.at[slot],
                    send_sem=sent, recv_sem=came, device_id=k, device_id_type=LOGICAL,
                ).start()

        got[pl.ds(slot, 1)] = z[pl.ds(slot, 1)]

    with jax.named_scope("f_fill"):
        lax.fori_loop(early, chunks, fill_v, 0)
        lax.fori_loop(0, chunks, fill_u, 0)

    with jax.named_scope("g_wait"):
        others = pl.ds(0, nx * ny - 1)
        every = pltpu.make_async_remote_copy(
            src_ref=z.at[others], dst_ref=got.at[others], send_sem=sent, recv_sem=came,
            device_id=me, device_id_type=LOGICAL,
        )
        every.wait_recv()

    with jax.named_scope("k_swap"):
        sums = split(
            jnp.concatenate(
                [
                    rolled(part, (ny - p) % ny * rq)
                    for c in range(2)
                    for p, part in enumerate(
                        pick_blocks([got[v * nx : (v + 1) * nx, c, :] for v in range(ny)], rq)
                    )
                ]
            )
        )
    with jax.named_scope("k_h"):
        both = mm3((ry[:, :hy], ry[:, hy:]), sums, NT)
        h_re = both[:ky, :hx] - both[ky:, hx:]
        h_im = both[:ky, hx:] + both[ky:, :hx]
        h = split(
            jnp.concatenate(
                [jnp.concatenate([h_re, -h_im], axis=1), jnp.concatenate([h_im, h_re], axis=1)],
                axis=0,
            )
        )
    with jax.named_scope("k_g2"):
        g = mm3(h, (rx[0], rx[1]), NN)
        high, low = split(g)
        copy_of = lax.broadcasted_iota(jnp.int32, g.shape, 1) // kx
        g = jnp.where(copy_of == 1, low.astype(F32), high.astype(F32)).astype(BF)
        live = counts[...]

    def degrid(j, carry):
        at = pl.ds(pl.multiple_of(j * wide, wide), wide)
        sums = mm(g, wu[:, at], NN)
        w = wv[:, at]
        block = (lax.broadcasted_iota(jnp.int32, (1, wide), 1) + j * wide) // VBLOCK
        alive = block < live
        re = jnp.sum(sums[:ky] * w, axis=0, keepdims=True)
        im = jnp.sum(sums[ky:] * w, axis=0, keepdims=True)
        out_ref[0, 0, :, at] = jnp.where(alive, re, 0.0)
        out_ref[1, 0, :, at] = jnp.where(alive, im, 0.0)
        return carry

    with jax.named_scope("l_degrid"):
        lax.fori_loop(0, nvis // wide, degrid, 0, unroll=4)
    with jax.named_scope("m_sent"):
        every.wait_send()


def solution(mesh):
    nx = mesh.shape["fx"]
    ny = mesh.shape["fy"]
    rp, rq = 16, 8

    def per_device(facets, counts, cells, fracs):
        rows, cols = facets.shape
        nvis = cells.shape[3]
        turn_x, right_x, win_x, back_x = axis_tables(nx, rows, nx, rp)
        turn_y, right_y, win_y, back_y = axis_tables(ny, cols, ny, rq)
        tx = jnp.asarray(np.concatenate([turn_x, right_x, win_x]), F32)
        ty = jnp.asarray(np.concatenate([turn_y, right_y, win_y]), F32)
        back_x = back_x.reshape(SUB, nx, rp).swapaxes(1, 2).reshape(SUB, nx * rp)
        base_x, re_x, im_x = compress(back_x, RANK_X)
        base_y, re_y, im_y = compress(back_y, RANK_Y)
        cell = halves(np.concatenate([base_x.T, base_y.T]), 1)
        rx = np.concatenate([re_x, im_x], axis=1).T
        rx = halves(np.concatenate([rx, rx, rx], axis=1)[None], 0)
        ry = halves(np.concatenate([re_y, im_y]), 1)
        hx, hy = nx * rp, ny * rq
        any_spec = pl.BlockSpec(memory_space=pltpu.HBM)
        dma = pltpu.SemaphoreType.DMA
        return pl.pallas_call(
            functools.partial(kernel, nx, ny, rp, rq),
            out_shape=pltpu.VMEM((2, 1, 1, nvis), F32),
            in_specs=[any_spec] * 9,
            out_specs=pl.BlockSpec(memory_space=pltpu.VMEM),
            scratch_shapes=[
                pltpu.VMEM(tx.shape, F32),
                pltpu.VMEM(ty.shape, F32),
                pltpu.VMEM(cell.shape, BF),
                pltpu.VMEM(rx.shape, BF),
                pltpu.VMEM(ry.shape, BF),
                pltpu.VMEM((rows, cols), F32),
                pltpu.VMEM((1, 1), jnp.int32),
                pltpu.VMEM(cells.shape, jnp.int32),
                pltpu.VMEM(fracs.shape, F32),
                pltpu.VMEM((2 * hy, cols), F32),
                pltpu.VMEM((nx * ny, 2, hy), F32),
                pltpu.VMEM((nx * ny, 2, hy), F32),
                pltpu.VMEM((3 * RANK_X, nvis), BF),
                pltpu.VMEM((RANK_Y, nvis), F32),
                dma((4,)),
                dma((8,)),
                dma,
                dma,
            ],
            compiler_params=pltpu.CompilerParams(
                collective_id=0, has_side_effects=True
            ),
        )(tx, ty, cell, rx, ry, facets, counts, cells, fracs)

    spec = P(None, "fx", "fy", None)
    return jax.shard_map(
        per_device,
        mesh=mesh,
        in_specs=(P("fx", "fy"), P("fx", "fy"), spec, spec),
        out_specs=spec,
        check_vma=False,
    )
```

```python
import functools
import math

import jax
import jax.numpy as jnp
import numpy as np
from jax import lax
from jax.experimental import pallas as pl
from jax.experimental.pallas import tpu as pltpu
from jax.sharding import PartitionSpec as P

NIMG = 65536
FP = 4096
SUB = 256
SUPPORT = 8
VBLOCK = 128
LOGICAL = pl.DeviceIdType.LOGICAL
BF = jnp.bfloat16
F32 = jnp.float32


def separable(cells, pixels, rank):
    a = np.arange(cells) - (cells - 1) / 2
    b = np.arange(pixels) - (pixels - 1) / 2
    theta = 2 * np.pi * np.outer(a, b) / NIMG
    half = rank // 2
    uc, sc, vc = np.linalg.svd(np.cos(theta), full_matrices=False)
    us, ss, vs = np.linalg.svd(np.sin(theta), full_matrices=False)
    left = np.concatenate([uc[:, :half] * sc[:half], -1j * us[:, :half] * ss[:half]], axis=1)
    right = np.concatenate([vc[:half], vs[:half]], axis=0)
    norm = math.sqrt(pixels)
    return left / norm, right * norm


def axis_tables(parts, pixels, subs, rank):
    left, right = separable(SUB, pixels, rank)
    right = right * math.sqrt(2.0 / (parts * pixels))
    xx = np.arange(pixels)
    mid = SUB * np.arange(subs) + (SUB - 1) / 2
    phase = 2 * np.pi * ((mid[:, None] * xx[None, :]) / NIMG)
    turn = np.concatenate([np.cos(phase), -np.sin(phase)], axis=0)
    x = np.arange(parts * pixels)
    window = np.sin(np.pi * ((x % FP) + 0.5) / FP).reshape(parts, pixels)
    kk = np.arange(SUB)
    at = (kk[:, None] * np.arange(parts)[None, :] * pixels % NIMG) / NIMG
    at = at + ((kk - (SUB - 1) / 2) * ((pixels - 1) / 2) / NIMG)[:, None]
    back = np.exp(-2j * np.pi * at)[:, :, None] * left[:, None, :]
    return turn, right, window, back.reshape(SUB, parts * rank)


def split(x):
    high = x.astype(BF)
    return high, (x - high.astype(F32)).astype(BF)


def halves(table, axis):
    table = table.astype(np.float32)
    high = table.astype(BF)
    low = (table - high.astype(np.float32)).astype(BF)
    return jnp.asarray(np.concatenate([high, low], axis=axis))


def mm(a, b, dims):
    return lax.dot_general(a, b, (dims, ((), ())), preferred_element_type=F32)


def mm3(a, b, dims):
    (ah, al), (bh, bl) = a, b
    return mm(ah, bh, dims) + (mm(ah, bl, dims) + mm(al, bh, dims))


NN = ((1,), (0,))
NT = ((1,), (1,))

WIDE = 512
RANK_X = 80
RANK_Y = 48


def place(k):
    return (k // 4 % 4, k // 64 * 2 + k // 2 % 2, k // 16 % 4, k % 2)


def hops(k):
    x, y, z, _ = place(k)
    return sum(min(c, 4 - c) for c in (x, y, z))


def launch_order(k):
    x, y, z, core = place(k)
    return ((z * 4 + y) * 4 + x, 1 - core)


SENDS = sorted(range(128), key=launch_order)
SIGNALS = sorted(range(128), key=lambda k: (-hops(k), launch_order(k)))


def compress(back, rank):
    terms = back.shape[1]
    u, s, v = np.linalg.svd(np.concatenate([back.real, back.imag], axis=1), full_matrices=False)
    rest = s[:rank, None] * v[:rank]
    return u[:, :rank], rest[:, :terms], rest[:, terms:]


def pick_blocks(parts, size):
    n = len(parts)
    block = lax.broadcasted_iota(jnp.int32, parts[0].shape, 1) // size
    d = 1
    while d < n:
        up = (block // d) % 2 == 1
        parts = [jnp.where(up, parts[(i + d) % n], parts[i]) for i in range(n)]
        d *= 2
    return [parts[-s % n] for s in range(n)]


def rolled(part, shift):
    return part if isinstance(shift, int) and shift == 0 else pltpu.roll(part, shift, 1)


def weights(offset, frac, shape):
    cell = lax.broadcasted_iota(jnp.int32, shape, 0).astype(F32)
    shift = cell - (offset.astype(F32) + (SUPPORT // 2 - 1))
    inside = jnp.abs(shift - 0.5) < SUPPORT // 2
    shift = shift - frac
    value = 0.6 * jnp.exp(shift * shift * (-1.0 / 4.5))
    return jnp.where(inside, value, 0.0)


def kernel(
    nx, ny, rp, rq, tx_hbm, ty_hbm, cell_hbm, rx_hbm, ry_hbm, f_hbm, counts_hbm, cells_hbm, fracs_hbm, out_ref,
    tx, ty, cell, rx, ry, f, counts, cells, fracs, m2, z, got, wu, wv,
    sent, came,
):
    me_x = lax.axis_index("fx")
    me_y = lax.axis_index("fy")
    rows = f.shape[0]
    cols = f.shape[1]
    step = rows // 4

    barrier = pltpu.get_barrier_semaphore()
    me = me_x * ny + me_y
    hx = nx * rp
    hy = ny * rq

    nvis = cells.shape[3]
    wide = WIDE
    kx = RANK_X
    ky = RANK_Y

    def fill_u(j, carry):
        at = pl.ds(pl.multiple_of(j * wide, wide), wide)
        w = split(weights(cells[0, 0, :, at], fracs[0, 0, :, at], (SUB, wide)))
        high, low = split(mm3((cell[:kx, :SUB], cell[:kx, SUB:]), w, NN))
        wu[:kx, at] = high
        wu[kx : 2 * kx, at] = high
        wu[2 * kx :, at] = low
        return carry

    def fill_v(j, carry):
        at = pl.ds(pl.multiple_of(j * wide, wide), wide)
        w = split(weights(cells[1, 0, :, at], fracs[1, 0, :, at], (SUB, wide)))
        wv[:, at] = mm3((cell[kx:, :SUB], cell[kx:, SUB:]), w, NN)
        return carry

    chunks = nvis // wide
    early = lax.div(3 - lax.rem(me_x, 4), 3) * chunks
    def front(fsem, lsem):
        small = [
            pltpu.make_async_copy(src, dst, lsem.at[i])
            for i, (src, dst) in enumerate(
                [
                    (tx_hbm, tx), (ty_hbm, ty), (cells_hbm, cells), (fracs_hbm, fracs),
                    (counts_hbm, counts), (cell_hbm, cell), (rx_hbm, rx), (ry_hbm, ry),
                ]
            )
        ]
        big = [
            pltpu.make_async_copy(
                f_hbm.at[pl.ds(i * step, step)], f.at[pl.ds(i * step, step)], fsem.at[i]
            )
            for i in range(4)
        ]
        with jax.named_scope("a_start"):
            small[0].start()
            big[0].start()
            small[1].start()
            for copy in big[1:] + small[2:]:
                copy.start()

            for i in range(0, len(SIGNALS), 16):
                group = SIGNALS[i : i + 16]

                def tell(k):
                    pl.semaphore_signal(barrier, inc=1, device_id=k, device_id_type=LOGICAL)

                mine = functools.reduce(jnp.logical_or, [me == k for k in group])

                @pl.when(jnp.logical_not(mine))
                def _():
                    for k in group:
                        tell(k)

                @pl.when(mine)
                def _():
                    for k in group:
                        pl.when(me != k)(functools.partial(tell, k))


        with jax.named_scope("b_c1"):
            small[0].wait()
            wx = tx[pl.ds(2 * nx + rp + me_x, 1), :]
            phi = tx[pl.ds(2 * nx, rp), :] * wx
            c1 = None
            for i in range(4):
                lanes = slice(i * step, (i + 1) * step)
                part = jnp.concatenate(
                    [
                        tx[c * nx : (c + 1) * nx, lanes] * phi[p : p + 1, lanes]
                        for c in range(2)
                        for p in range(rp)
                    ],
                    axis=0,
                )
                big[i].wait()
                prod = mm3(split(part), split(f[pl.ds(i * step, step), :]), NN)
                c1 = prod if c1 is None else c1 + prod

        with jax.named_scope("c_d"):
            small[1].wait()
            wy = ty[pl.ds(2 * ny + rq + me_y, 1), :]
            phi = ty[pl.ds(2 * ny, rq), :] * wy
            for r in range(2 * ny):
                m2[pl.ds(r * rq, rq), :] = jnp.broadcast_to(ty[pl.ds(r, 1), :], (rq, cols)) * phi
            prod = mm3(split(c1), split(m2[...]), NT)
            re = prod[:hx, :hy] - prod[hx:, hy:]
            im = prod[:hx, hy:] + prod[hx:, :hy]
            for c, part in enumerate((re, im)):
                swapped = pick_blocks(
                    [rolled(part[p * nx : (p + 1) * nx], p * rq) for p in range(rp)], rq
                )
                for v in range(ny):
                    turn = lax.rem(me_y + (ny - v), ny) * rq
                    z[v * nx : (v + 1) * nx, c, :] = rolled(swapped[v], turn)

        with jax.named_scope("c_fill"):
            for copy in small[2:]:
                copy.wait()
            lax.fori_loop(0, early, fill_v, 0)

    pl.run_scoped(front, pltpu.SemaphoreType.DMA((4,)), pltpu.SemaphoreType.DMA((8,)))

    with jax.named_scope("d_barrier"):
        pl.semaphore_wait(barrier, nx * ny - 1)
    with jax.named_scope("e_send"):
        slot = me_y * nx + me_x
        for k in SENDS:

            @pl.when(me != k)
            def _():
                pltpu.make_async_remote_copy(
                    src_ref=z.at[k % ny * nx + k // ny], dst_ref=got.at[slot],
                    send_sem=sent, recv_sem=came, device_id=k, device_id_type=LOGICAL,
                ).start()

        got[pl.ds(slot, 1)] = z[pl.ds(slot, 1)]

    with jax.named_scope("f_fill"):
        lax.fori_loop(early, chunks, fill_v, 0)
        lax.fori_loop(0, chunks, fill_u, 0)

    with jax.named_scope("g_wait"):
        others = pl.ds(0, nx * ny - 1)
        every = pltpu.make_async_remote_copy(
            src_ref=z.at[others], dst_ref=got.at[others], send_sem=sent, recv_sem=came,
            device_id=me, device_id_type=LOGICAL,
        )
        every.wait_recv()

    with jax.named_scope("k_swap"):
        sums = split(
            jnp.concatenate(
                [
                    rolled(part, (ny - p) % ny * rq)
                    for c in range(2)
                    for p, part in enumerate(
                        pick_blocks([got[v * nx : (v + 1) * nx, c, :] for v in range(ny)], rq)
                    )
                ]
            )
        )
    with jax.named_scope("k_h"):
        both = mm3((ry[:, :hy], ry[:, hy:]), sums, NT)
        h_re = both[:ky, :hx] - both[ky:, hx:]
        h_im = both[:ky, hx:] + both[ky:, :hx]
        h = split(
            jnp.concatenate(
                [jnp.concatenate([h_re, -h_im], axis=1), jnp.concatenate([h_im, h_re], axis=1)],
                axis=0,
            )
        )
    with jax.named_scope("k_g2"):
        g = mm3(h, (rx[0], rx[1]), NN)
        high, low = split(g)
        copy_of = lax.broadcasted_iota(jnp.int32, g.shape, 1) // kx
        g = jnp.where(copy_of == 1, low.astype(F32), high.astype(F32)).astype(BF)
        live = counts[...]

    def degrid(j, carry):
        at = pl.ds(pl.multiple_of(j * wide, wide), wide)
        sums = mm(g, wu[:, at], NN)
        w = wv[:, at]
        block = (lax.broadcasted_iota(jnp.int32, (1, wide), 1) + j * wide) // VBLOCK
        alive = block < live
        re = jnp.sum(sums[:ky] * w, axis=0, keepdims=True)
        im = jnp.sum(sums[ky:] * w, axis=0, keepdims=True)
        out_ref[0, 0, :, at] = jnp.where(alive, re, 0.0)
        out_ref[1, 0, :, at] = jnp.where(alive, im, 0.0)
        return carry

    with jax.named_scope("l_degrid"):
        lax.fori_loop(0, nvis // wide, degrid, 0, unroll=4)
    with jax.named_scope("m_sent"):
        every.wait_send()


def solution(mesh):
    nx = mesh.shape["fx"]
    ny = mesh.shape["fy"]
    rp, rq = 16, 8

    def per_device(facets, counts, cells, fracs):
        rows, cols = facets.shape
        nvis = cells.shape[3]
        turn_x, right_x, win_x, back_x = axis_tables(nx, rows, nx, rp)
        turn_y, right_y, win_y, back_y = axis_tables(ny, cols, ny, rq)
        tx = jnp.asarray(np.concatenate([turn_x, right_x, win_x]), F32)
        ty = jnp.asarray(np.concatenate([turn_y, right_y, win_y]), F32)
        back_x = back_x.reshape(SUB, nx, rp).swapaxes(1, 2).reshape(SUB, nx * rp)
        base_x, re_x, im_x = compress(back_x, RANK_X)
        base_y, re_y, im_y = compress(back_y, RANK_Y)
        cell = halves(np.concatenate([base_x.T, base_y.T]), 1)
        rx = np.concatenate([re_x, im_x], axis=1).T
        rx = halves(np.concatenate([rx, rx, rx], axis=1)[None], 0)
        ry = halves(np.concatenate([re_y, im_y]), 1)
        hx, hy = nx * rp, ny * rq
        any_spec = pl.BlockSpec(memory_space=pltpu.HBM)
        dma = pltpu.SemaphoreType.DMA
        return pl.pallas_call(
            functools.partial(kernel, nx, ny, rp, rq),
            out_shape=pltpu.VMEM((2, 1, 1, nvis), F32),
            in_specs=[any_spec] * 9,
            out_specs=pl.BlockSpec(memory_space=pltpu.VMEM),
            scratch_shapes=[
                pltpu.VMEM(tx.shape, F32),
                pltpu.VMEM(ty.shape, F32),
                pltpu.VMEM(cell.shape, BF),
                pltpu.VMEM(rx.shape, BF),
                pltpu.VMEM(ry.shape, BF),
                pltpu.VMEM((rows, cols), F32),
                pltpu.VMEM((1, 1), jnp.int32),
                pltpu.VMEM(cells.shape, jnp.int32),
                pltpu.VMEM(fracs.shape, F32),
                pltpu.VMEM((2 * hy, cols), F32),
                pltpu.VMEM((nx * ny, 2, hy), F32),
                pltpu.VMEM((nx * ny, 2, hy), F32),
                pltpu.VMEM((3 * RANK_X, nvis), BF),
                pltpu.VMEM((RANK_Y, nvis), F32),
                dma,
                dma,
            ],
            compiler_params=pltpu.CompilerParams(
                collective_id=0, has_side_effects=True
            ),
        )(tx, ty, cell, rx, ry, facets, counts, cells, fracs)

    spec = P(None, "fx", "fy", None)
    return jax.shard_map(
        per_device,
        mesh=mesh,
        in_specs=(P("fx", "fy"), P("fx", "fy"), spec, spec),
        out_specs=spec,
        check_vma=False,
    )
```

```python
import functools
import math

import jax
import jax.numpy as jnp
import numpy as np
from jax import lax
from jax.experimental import pallas as pl
from jax.experimental.pallas import tpu as pltpu
from jax.sharding import PartitionSpec as P

NIMG = 65536
FP = 4096
SUB = 256
SUPPORT = 8
VBLOCK = 128
LOGICAL = pl.DeviceIdType.LOGICAL
BF = jnp.bfloat16
F32 = jnp.float32


def separable(cells, pixels, rank):
    a = np.arange(cells) - (cells - 1) / 2
    b = np.arange(pixels) - (pixels - 1) / 2
    theta = 2 * np.pi * np.outer(a, b) / NIMG
    half = rank // 2
    uc, sc, vc = np.linalg.svd(np.cos(theta), full_matrices=False)
    us, ss, vs = np.linalg.svd(np.sin(theta), full_matrices=False)
    left = np.concatenate([uc[:, :half] * sc[:half], -1j * us[:, :half] * ss[:half]], axis=1)
    right = np.concatenate([vc[:half], vs[:half]], axis=0)
    norm = math.sqrt(pixels)
    return left / norm, right * norm


def axis_tables(parts, pixels, subs, rank):
    left, right = separable(SUB, pixels, rank)
    right = right * math.sqrt(2.0 / (parts * pixels))
    xx = np.arange(pixels)
    mid = SUB * np.arange(subs) + (SUB - 1) / 2
    phase = 2 * np.pi * ((mid[:, None] * xx[None, :]) / NIMG)
    turn = np.concatenate([np.cos(phase), -np.sin(phase)], axis=0)
    x = np.arange(parts * pixels)
    window = np.sin(np.pi * ((x % FP) + 0.5) / FP).reshape(parts, pixels)
    kk = np.arange(SUB)
    at = (kk[:, None] * np.arange(parts)[None, :] * pixels % NIMG) / NIMG
    at = at + ((kk - (SUB - 1) / 2) * ((pixels - 1) / 2) / NIMG)[:, None]
    back = np.exp(-2j * np.pi * at)[:, :, None] * left[:, None, :]
    return turn, right, window, back.reshape(SUB, parts * rank)


def split(x):
    high = x.astype(BF)
    return high, (x - high.astype(F32)).astype(BF)


def halves(table, axis):
    table = table.astype(np.float32)
    high = table.astype(BF)
    low = (table - high.astype(np.float32)).astype(BF)
    return jnp.asarray(np.concatenate([high, low], axis=axis))


def mm(a, b, dims):
    return lax.dot_general(a, b, (dims, ((), ())), preferred_element_type=F32)


def mm3(a, b, dims):
    (ah, al), (bh, bl) = a, b
    return mm(ah, bh, dims) + (mm(ah, bl, dims) + mm(al, bh, dims))


NN = ((1,), (0,))
NT = ((1,), (1,))

WIDE = 512
RANK_X = 80
RANK_Y = 48


def place(k):
    return (k // 4 % 4, k // 64 * 2 + k // 2 % 2, k // 16 % 4, k % 2)


def hops(k):
    x, y, z, _ = place(k)
    return sum(min(c, 4 - c) for c in (x, y, z))


def launch_order(k):
    x, y, z, core = place(k)
    return ((z * 4 + y) * 4 + x, 1 - core)


SENDS = sorted(range(128), key=launch_order)
SIGNALS = sorted(range(128), key=lambda k: (-hops(k), launch_order(k)))


def compress(back, rank):
    terms = back.shape[1]
    u, s, v = np.linalg.svd(np.concatenate([back.real, back.imag], axis=1), full_matrices=False)
    rest = s[:rank, None] * v[:rank]
    return u[:, :rank], rest[:, :terms], rest[:, terms:]


def pick_blocks(parts, size):
    n = len(parts)
    block = lax.broadcasted_iota(jnp.int32, parts[0].shape, 1) // size
    d = 1
    while d < n:
        up = (block // d) % 2 == 1
        parts = [jnp.where(up, parts[(i + d) % n], parts[i]) for i in range(n)]
        d *= 2
    return [parts[-s % n] for s in range(n)]


def rolled(part, shift):
    return part if isinstance(shift, int) and shift == 0 else pltpu.roll(part, shift, 1)


def weights(offset, frac, shape):
    cell = lax.broadcasted_iota(jnp.int32, shape, 0).astype(F32)
    shift = cell - (offset.astype(F32) + (SUPPORT // 2 - 1))
    inside = jnp.abs(shift - 0.5) < SUPPORT // 2
    shift = shift - frac
    value = 0.6 * jnp.exp(shift * shift * (-1.0 / 4.5))
    return jnp.where(inside, value, 0.0)


def kernel(
    nx, ny, rp, rq, tx_hbm, ty_hbm, cell_hbm, rx_hbm, ry_hbm, f_hbm, counts_hbm, cells_hbm, fracs_hbm, out_ref,
    tx, ty, cell, rx, ry, f, counts, cells, fracs, m2, z, got, wu, wv,
    sent, came,
):
    me_x = lax.axis_index("fx")
    me_y = lax.axis_index("fy")
    rows = f.shape[0]
    cols = f.shape[1]
    step = rows // 4

    barrier = pltpu.get_barrier_semaphore()
    me = me_x * ny + me_y
    hx = nx * rp
    hy = ny * rq

    nvis = cells.shape[3]
    wide = WIDE
    kx = RANK_X
    ky = RANK_Y

    def fill_u(j, carry):
        at = pl.ds(pl.multiple_of(j * wide, wide), wide)
        w = split(weights(cells[0, 0, :, at], fracs[0, 0, :, at], (SUB, wide)))
        high, low = split(mm3((cell[:kx, :SUB], cell[:kx, SUB:]), w, NN))
        wu[:kx, at] = high
        wu[kx : 2 * kx, at] = high
        wu[2 * kx :, at] = low
        return carry

    def fill_v(j, carry):
        at = pl.ds(pl.multiple_of(j * wide, wide), wide)
        w = split(weights(cells[1, 0, :, at], fracs[1, 0, :, at], (SUB, wide)))
        wv[:, at] = mm3((cell[kx:, :SUB], cell[kx:, SUB:]), w, NN)
        return carry

    chunks = nvis // wide
    early = lax.div(3 - lax.rem(me_x, 4), 3) * chunks
    def front(fsem, lsem):
        small = [
            pltpu.make_async_copy(src, dst, lsem.at[i])
            for i, (src, dst) in enumerate(
                [
                    (tx_hbm, tx), (ty_hbm, ty), (cells_hbm, cells), (fracs_hbm, fracs),
                    (counts_hbm, counts), (cell_hbm, cell), (rx_hbm, rx), (ry_hbm, ry),
                ]
            )
        ]
        big = [
            pltpu.make_async_copy(
                f_hbm.at[pl.ds(i * step, step)], f.at[pl.ds(i * step, step)], fsem.at[i]
            )
            for i in range(4)
        ]
        with jax.named_scope("a_start"):
            small[0].start()
            big[0].start()
            small[1].start()
            for copy in big[1:] + small[2:]:
                copy.start()

            for k in SIGNALS:

                @pl.when(me != k)
                def _():
                    pl.semaphore_signal(barrier, inc=1, device_id=k, device_id_type=LOGICAL)

        with jax.named_scope("b_c1"):
            small[0].wait()
            wx = tx[pl.ds(2 * nx + rp + me_x, 1), :]
            phi = tx[pl.ds(2 * nx, rp), :] * wx
            c1 = None
            for i in range(4):
                lanes = slice(i * step, (i + 1) * step)
                part = jnp.concatenate(
                    [
                        tx[c * nx : (c + 1) * nx, lanes] * phi[p : p + 1, lanes]
                        for c in range(2)
                        for p in range(rp)
                    ],
                    axis=0,
                )
                big[i].wait()
                prod = mm3(split(part), split(f[pl.ds(i * step, step), :]), NN)
                c1 = prod if c1 is None else c1 + prod

        with jax.named_scope("c_d"):
            small[1].wait()
            wy = ty[pl.ds(2 * ny + rq + me_y, 1), :]
            phi = ty[pl.ds(2 * ny, rq), :] * wy
            for r in range(2 * ny):
                m2[pl.ds(r * rq, rq), :] = jnp.broadcast_to(ty[pl.ds(r, 1), :], (rq, cols)) * phi
            prod = mm3(split(c1), split(m2[...]), NT)
            re = prod[:hx, :hy] - prod[hx:, hy:]
            im = prod[:hx, hy:] + prod[hx:, :hy]
            for c, part in enumerate((re, im)):
                swapped = pick_blocks(
                    [rolled(part[p * nx : (p + 1) * nx], p * rq) for p in range(rp)], rq
                )
                for v in range(ny):
                    turn = lax.rem(me_y + (ny - v), ny) * rq
                    z[v * nx : (v + 1) * nx, c, :] = rolled(swapped[v], turn)

        with jax.named_scope("c_fill"):
            for copy in small[2:]:
                copy.wait()
            lax.fori_loop(0, early, fill_v, 0)

    pl.run_scoped(front, pltpu.SemaphoreType.DMA((4,)), pltpu.SemaphoreType.DMA((8,)))

    with jax.named_scope("d_barrier"):
        pl.semaphore_wait(barrier, nx * ny - 1)
    with jax.named_scope("e_send"):
        slot = me_y * nx + me_x
        for k in SENDS:

            @pl.when(me != k)
            def _():
                pltpu.make_async_remote_copy(
                    src_ref=z.at[k % ny * nx + k // ny], dst_ref=got.at[slot],
                    send_sem=sent, recv_sem=came, device_id=k, device_id_type=LOGICAL,
                ).start()

        got[pl.ds(slot, 1)] = z[pl.ds(slot, 1)]

    with jax.named_scope("f_fill"):
        lax.fori_loop(early, chunks, fill_v, 0)
        lax.fori_loop(0, chunks, fill_u, 0)

    with jax.named_scope("g_wait"):
        others = pl.ds(0, nx * ny - 1)
        every = pltpu.make_async_remote_copy(
            src_ref=z.at[others], dst_ref=got.at[others], send_sem=sent, recv_sem=came,
            device_id=me, device_id_type=LOGICAL,
        )
        every.wait_recv()

    with jax.named_scope("k_swap"):
        sums = split(
            jnp.concatenate(
                [
                    rolled(part, (ny - p) % ny * rq)
                    for c in range(2)
                    for p, part in enumerate(
                        pick_blocks([got[v * nx : (v + 1) * nx, c, :] for v in range(ny)], rq)
                    )
                ]
            )
        )
    with jax.named_scope("k_h"):
        both = mm3((ry[:, :hy], ry[:, hy:]), sums, NT)
        h_re = both[:ky, :hx] - both[ky:, hx:]
        h_im = both[:ky, hx:] + both[ky:, :hx]
        h = split(
            jnp.concatenate(
                [jnp.concatenate([h_re, -h_im], axis=1), jnp.concatenate([h_im, h_re], axis=1)],
                axis=0,
            )
        )
    with jax.named_scope("k_g2"):
        g = mm3(h, (rx[0], rx[1]), NN)
        high, low = split(g)
        copy_of = lax.broadcasted_iota(jnp.int32, g.shape, 1) // kx
        g = jnp.where(copy_of == 1, low.astype(F32), high.astype(F32)).astype(BF)
        live = counts[...]

    def degrid(j, carry):
        at = pl.ds(pl.multiple_of(j * wide, wide), wide)
        sums = mm(g, wu[:, at], NN)
        w = wv[:, at]
        block = (lax.broadcasted_iota(jnp.int32, (1, wide), 1) + j * wide) // VBLOCK
        alive = block < live
        re = jnp.sum(sums[:ky] * w, axis=0, keepdims=True)
        im = jnp.sum(sums[ky:] * w, axis=0, keepdims=True)
        out_ref[0, 0, :, at] = jnp.where(alive, re, 0.0)
        out_ref[1, 0, :, at] = jnp.where(alive, im, 0.0)
        return carry

    with jax.named_scope("l_degrid"):
        lax.fori_loop(0, nvis // wide, degrid, 0, unroll=4)
    with jax.named_scope("m_sent"):
        every.wait_send()


def solution(mesh):
    nx = mesh.shape["fx"]
    ny = mesh.shape["fy"]
    rp, rq = 16, 8

    def per_device(facets, counts, cells, fracs):
        rows, cols = facets.shape
        nvis = cells.shape[3]
        turn_x, right_x, win_x, back_x = axis_tables(nx, rows, nx, rp)
        turn_y, right_y, win_y, back_y = axis_tables(ny, cols, ny, rq)
        tx = jnp.asarray(np.concatenate([turn_x, right_x, win_x]), F32)
        ty = jnp.asarray(np.concatenate([turn_y, right_y, win_y]), F32)
        back_x = back_x.reshape(SUB, nx, rp).swapaxes(1, 2).reshape(SUB, nx * rp)
        base_x, re_x, im_x = compress(back_x, RANK_X)
        base_y, re_y, im_y = compress(back_y, RANK_Y)
        cell = halves(np.concatenate([base_x.T, base_y.T]), 1)
        rx = np.concatenate([re_x, im_x], axis=1).T
        rx = halves(np.concatenate([rx, rx, rx], axis=1)[None], 0)
        ry = halves(np.concatenate([re_y, im_y]), 1)
        hx, hy = nx * rp, ny * rq
        any_spec = pl.BlockSpec(memory_space=pltpu.HBM)
        dma = pltpu.SemaphoreType.DMA
        return pl.pallas_call(
            functools.partial(kernel, nx, ny, rp, rq),
            out_shape=pltpu.VMEM((2, 1, 1, nvis), F32),
            in_specs=[any_spec] * 9,
            out_specs=pl.BlockSpec(memory_space=pltpu.VMEM),
            scratch_shapes=[
                pltpu.VMEM(tx.shape, F32),
                pltpu.VMEM(ty.shape, F32),
                pltpu.VMEM(cell.shape, BF),
                pltpu.VMEM(rx.shape, BF),
                pltpu.VMEM(ry.shape, BF),
                pltpu.VMEM((rows, cols), F32),
                pltpu.VMEM((1, 1), jnp.int32),
                pltpu.VMEM(cells.shape, jnp.int32),
                pltpu.VMEM(fracs.shape, F32),
                pltpu.VMEM((2 * hy, cols), F32),
                pltpu.VMEM((nx * ny, 2, hy), F32),
                pltpu.VMEM((nx * ny, 2, hy), F32),
                pltpu.VMEM((3 * RANK_X, nvis), BF),
                pltpu.VMEM((RANK_Y, nvis), F32),
                dma,
                dma,
            ],
            compiler_params=pltpu.CompilerParams(
                collective_id=0, has_side_effects=True
            ),
        )(tx, ty, cell, rx, ry, facets, counts, cells, fracs)

    spec = P(None, "fx", "fy", None)
    return jax.shard_map(
        per_device,
        mesh=mesh,
        in_specs=(P("fx", "fy"), P("fx", "fy"), spec, spec),
        out_specs=spec,
        check_vma=False,
    )
```
